512 devices in a mesh: rows: 16 (over z, y_lo), feat: 8 (over x, core), leaf: 4 (over y_hi).
Axes of the slice: x: 4, y: 8 (y_hi: 4, y_lo: 2; y = y_hi * 2 + y_lo), z: 8, core: 2. Of those that a mesh axis runs over, the one named last changes fastest.
Arguments:
- features: float32 [512, 32768], P(None, ('rows', 'feat')), may hold values from -4 to 4
- labels: int32 [32768], P(('rows', 'feat')), may hold values from 0 to 63
- weights: bfloat16 [4, 32768], P('leaf', ('rows', 'feat')), may hold values from 0.0009994507 to 4
- nodes: int32 [4, 32768], P('leaf', ('rows', 'feat')), may hold values from 0 to 1
Outputs:
- split_gain: float32 [4, 2, 512], P('leaf', None, ('rows', 'feat'))
- node_best: float32 [4, 2], P('leaf')
The draws below stay inside these ranges and needn't reach their ends.
All inputs are finite; a program needn't handle non-finite values.
Results may differ from the reference program's by a relative error of at most 0.0003.
Values may be sent and summed in bfloat16 or wider, within the bound.
A program may use at most 64 MiB of HBM per device.

```python
import math
import jax
import jax.numpy as jnp
from jax import lax

F = 512
B = 128
C = 64
NODES = 2
TREES = 4
ROWS = 32768


def place_ends(values, rng, low, largest):
    longest = values.shape.index(max(values.shape))
    spots = []
    for shift in (0, 1):
        where = [jax.random.randint(jax.random.fold_in(rng, axis), (), 0, length) for axis, length in enumerate(values.shape)]
        where[longest] = (where[longest] + shift) % values.shape[longest]
        spots.append(tuple(where))
    return values.at[spots[0]].set(low).at[spots[1]].set(largest)


def block_levels(own_key, extent, split, smallest, largest):
    def one(axis_at, parts):
        heights = jax.random.uniform(jax.random.fold_in(jax.random.fold_in(own_key, 6), axis_at), (parts,), jnp.float32, smallest / len(split), largest / len(split))
        return jnp.repeat(jnp.exp(heights), extent[axis_at] // parts).reshape((-1,) + (1,) * (len(extent) - axis_at - 1))

    level = one(*split[0])
    for cut in split[1:]:
        level = level * one(*cut)
    return level


def normal_values(stream_key, shape, spread, most, pieces=(), held_as=jnp.bfloat16):
    entries = jax.random.normal(stream_key, shape, jnp.float32) * spread
    if len(pieces) > 0:
        entries = block_levels(stream_key, shape, pieces, -0.22, 0.18) * entries
    return jnp.clip(entries, min=-most, max=most).astype(held_as)


def setup_inputs(seed: int = 0) -> dict:
    seeds = jax.random.split(jax.random.key(seed), 5)
    return {
        "features": normal_values(seeds[0], (F, ROWS), 1.0, 4.0, ((1, 128),), jnp.float32),
        "labels": place_ends(jax.random.randint(seeds[1], (ROWS,), 0, C), jax.random.fold_in(seeds[1], 1), 0, C - 1).astype(jnp.int32),
        "weights": jnp.clip(jnp.exp(math.log(4.0) - 8.2946 * jax.random.uniform(seeds[2], (TREES, ROWS), jnp.float32) ** block_levels(seeds[2], (TREES, ROWS), ((0, 4), (1, 128)), -0.2, 0.2)), 0.0009994507, 4.0).astype(jnp.bfloat16),
        "nodes": place_ends(jax.random.randint(seeds[3], (TREES, ROWS), 0, NODES), jax.random.fold_in(seeds[3], 1), 0, NODES - 1).astype(jnp.int32),
    }


def edge_table(bin_count, dtype):
    positions = jnp.arange(bin_count - 1, dtype=dtype)
    return (positions + 1.0 - bin_count // 2) * (9.0 / bin_count)


def split_scores(cumulative):
    totals = cumulative[..., -1:, :, :]
    right_side = totals - cumulative

    def ratio_sum(values):
        return jnp.sum(values * values, axis=-1) / jnp.maximum(jnp.sum(values, axis=-1), 1.0)

    split_value = ratio_sum(cumulative) + ratio_sum(right_side) - ratio_sum(totals)
    return jnp.max(split_value, axis=-2)


def reference(features, labels, weights, nodes):
    edge_values = edge_table(B, jnp.float32)
    group_count = TREES * NODES * C
    tree_index = jnp.arange(TREES, dtype=jnp.int32)[:, None]
    group_index = ((tree_index * NODES + nodes) * C + labels[None, :]).astype(jnp.int32)
    weight_values = weights.astype(jnp.float32).reshape(-1)

    def per_column(column):
        bin_index = jnp.searchsorted(edge_values, column, side="left").astype(jnp.int32)
        flat_index = (bin_index[None, :] * group_count + group_index).astype(jnp.int32)
        counts = jnp.zeros((B * group_count,), jnp.float32).at[flat_index.reshape(-1)].add(weight_values)
        cumulative = jnp.cumsum(counts.reshape(B, TREES * NODES, C), axis=0)
        return split_scores(cumulative)

    scores = lax.map(per_column, features)
    split_gain = scores.T.reshape(TREES, NODES, F)
    node_best = jnp.max(split_gain, axis=2)
    return split_gain, node_best
```

```python
import functools

import jax
import jax.numpy as jnp
from jax import lax
from jax.experimental import pallas as pl
from jax.experimental.pallas import tpu as pltpu
from jax.sharding import PartitionSpec as P

B = 128
C = 64
NODES = 2
OWN = 4
Z = 8
Y = 2
X = 4
CORES = 2
ROWS_AX = Z * Y
FEAT_AX = X * CORES
LOCAL = 256
GROUP = 2
f32 = jnp.float32
bf16 = jnp.bfloat16
MESH = pl.DeviceIdType.MESH
NT = (((1,), (1,)), ((), ()))
ORDER = [(0, 0), (0, 1), (1, 0), (7, 0), (1, 1), (7, 1), (2, 0), (6, 0), (2, 1), (6, 1), (3, 0), (5, 0), (3, 1), (5, 1), (4, 0), (4, 1)]


def bin_index(x):
    guess = jnp.clip(jnp.ceil(x * (B / 9.0) + (B // 2 - 1)), 0.0, B - 1.0)
    edge_here = (guess + (1.0 - B // 2)) * (9.0 / B)
    edge_before = (guess - (1.0 * (B // 2))) * (9.0 / B)
    up = jnp.where((edge_here < x) & (guess < B - 1.0), 1.0, 0.0)
    down = jnp.where((edge_before >= x) & (guess > 0.0), 1.0, 0.0)
    return guess + up - down


def row_pack(tile, row):
    return jnp.broadcast_to(tile[row : row + 1, :], (16, 128)).astype(bf16)


def mask_tile(tile, bins):
    one, zero = jnp.ones((), bf16), jnp.zeros((), bf16)
    rows = []
    for i in range(OWN):
        halves = []
        for h in range(2):
            packed = row_pack(tile, h * 4 + i)
            halves.append(jnp.where(packed[None] <= bins, one, zero).reshape(B, 128))
        rows.append(jnp.concatenate(halves, axis=1))
    return jnp.concatenate(rows, axis=0)


def target_tile(tile, classes):
    zero = jnp.zeros((), bf16)
    parts = [[], []]
    for h in range(2):
        hit = row_pack(tile, h * 4)[None] == classes
        for n in range(NODES):
            weight = jnp.broadcast_to(row_pack(tile, h * 4 + 1 + n)[None], hit.shape)
            parts[n].append(jnp.where(hit, weight, zero).reshape(C, 128))
    return jnp.concatenate([jnp.concatenate(p, axis=1) for p in parts], axis=0)


def ratio(values):
    return jnp.sum(values * values, axis=0, keepdims=True) / jnp.maximum(jnp.sum(values, axis=0, keepdims=True), 1.0)


def kernel(
    feat_hbm, lab_ref, wei_ref, node_ref, gain_ref, best_ref,
    feat_v, send, own_codes, zbuf, zcode, rbuf, rcode, acc, m1s, m1, m2s, m2,
    in_sem, s1_send, s1_recv, c1_send, c1_recv, s2_send, s2_recv, c2_send, c2_recv, m1_send, m1_recv, m2_send, m2_recv,
):
    my_rows, my_feat = lax.axis_index("rows"), lax.axis_index("feat")
    z, y = lax.div(my_rows, Y), lax.rem(my_rows, Y)
    loads = []
    for q in range(4):
        part = pl.ds(q * 128, 128)
        loads.append(pltpu.make_async_copy(feat_hbm.at[part], feat_v.at[part], in_sem.at[q]))
        loads[-1].start()

    def rows_peer(dz, dy):
        return lax.rem(z + dz, Z) * Y + lax.rem(y + dy, Y)

    def feat_peer(d):
        return lax.rem(my_feat + d, FEAT_AX)

    barrier = pltpu.get_barrier_semaphore()
    for dz, dy in ORDER[1:]:
        pl.semaphore_signal(barrier, inc=1, device_id={"rows": rows_peer(dz, dy)}, device_id_type=MESH)
    for d in range(1, FEAT_AX):
        pl.semaphore_signal(barrier, inc=1, device_id={"feat": feat_peer(d)}, device_id_type=MESH)

    label = lab_ref[...].astype(f32)
    weight = wei_ref[...].astype(f32)
    node = node_ref[...]
    w0 = jnp.where(node == 0, weight, 0.0)
    w1 = jnp.where(node == 1, weight, 0.0)
    pad = jnp.zeros_like(w0)
    lines = []
    for h in range(2):
        cut = slice(h * 128, (h + 1) * 128)
        lines += [label[:, cut], w0[:, cut], w1[:, cut], pad[:, cut]]
    own_codes[...] = jnp.concatenate(lines, axis=0).astype(bf16)

    sub = lax.broadcasted_iota(jnp.int32, (4, 8, 128), 1)
    for q in range(4):
        loads[q].wait()

        def place(r, carry):
            values = bin_index(feat_v[pl.ds(pl.multiple_of(r * 32, 32), 32), :])
            a = values[:, :128].reshape(4, 8, 128)
            b = values[:, 128:].reshape(4, 8, 128)
            first = jnp.where(sub < 4, a, pltpu.roll(b, 4, 1))
            second = jnp.where(sub < 4, pltpu.roll(a, 4, 1), b)
            both = jnp.stack([first, second], axis=1).reshape(8, 8, 128)
            send[r] = both.astype(bf16)
            return carry

        lax.fori_loop(q * 4, q * 4 + 4, place, 0)

    pl.semaphore_wait(barrier, ROWS_AX - 1 + FEAT_AX - 1)

    first_copies = {}
    for s in range(1, ROWS_AX):
        peer = rows_peer(*ORDER[s])
        first_copies[s] = (
            pltpu.make_async_remote_copy(
                src_ref=send.at[peer], dst_ref=zbuf.at[s], send_sem=s1_send.at[s], recv_sem=s1_recv.at[s],
                device_id={"rows": peer}, device_id_type=MESH),
            pltpu.make_async_remote_copy(
                src_ref=own_codes, dst_ref=zcode.at[s], send_sem=c1_send.at[s], recv_sem=c1_recv.at[s],
                device_id={"rows": peer}, device_id_type=MESH),
        )
        for copy in first_copies[s]:
            copy.start()

    def forward(s):
        if s > 0:
            for copy in first_copies[s]:
                copy.wait_recv()
        for d in range(1, FEAT_AX):
            peer = feat_peer(d)
            source = zbuf.at[s, peer] if s > 0 else send.at[my_rows, peer]
            pltpu.make_async_remote_copy(
                src_ref=source, dst_ref=rbuf.at[s, d], send_sem=s2_send.at[s], recv_sem=s2_recv.at[s],
                device_id={"feat": peer}, device_id_type=MESH).start()
            pltpu.make_async_remote_copy(
                src_ref=zcode.at[s] if s > 0 else own_codes, dst_ref=rcode.at[s, d], send_sem=c2_send.at[s], recv_sem=c2_recv.at[s],
                device_id={"feat": peer}, device_id_type=MESH).start()

    def all_of(buffer, s, sem):
        part = buffer.at[s, pl.ds(1, FEAT_AX - 1)]
        return pltpu.make_async_copy(part, part, sem.at[s])

    bins = (lax.broadcasted_iota(jnp.int32, (8, 16, 128), 0) * 16 + lax.broadcasted_iota(jnp.int32, (8, 16, 128), 1)).astype(f32).astype(bf16)
    classes = bins[: C // 16]
    acc[...] = jnp.zeros_like(acc)

    def use(slots):
        masks, targets = [], []
        for s in slots:
            all_of(rbuf, s, s2_recv).wait()
            all_of(rcode, s, c2_recv).wait()
        for s in slots:
            mine = zbuf[s, my_feat] if s > 0 else send[my_rows, my_feat]
            codes = zcode[s] if s > 0 else own_codes[...]
            masks.append(mask_tile(mine.astype(f32), bins))
            targets.append(target_tile(codes.astype(f32), classes))
            for d in range(1, FEAT_AX):
                masks.append(mask_tile(rbuf[s, d].astype(f32), bins))
                targets.append(target_tile(rcode[s, d].astype(f32), classes))
        acc[...] += lax.dot_general(jnp.concatenate(masks, axis=1), jnp.concatenate(targets, axis=1), NT, preferred_element_type=f32)

    groups = [list(range(g, g + GROUP)) for g in range(0, ROWS_AX, GROUP)]
    for g, slots in enumerate(groups):
        for s in slots:
            forward(s)
        if g >= 1:
            use(groups[g - 1])
    use(groups[-1])

    row_at = lax.broadcasted_iota(jnp.int32, (8, 128), 0)
    lane_at = lax.broadcasted_iota(jnp.int32, (8, 128), 1)
    gains = jnp.zeros((8, 128), f32)
    best = jnp.zeros((8, 128), f32)
    for n in range(NODES):
        node_top = None
        for i in range(OWN):
            left = acc[i * B : (i + 1) * B, :].T[n * C : (n + 1) * C, :]
            total = left[:, B - 1 : B]
            right = total - left
            gain = ratio(left) + ratio(right) - ratio(total)
            top = jnp.max(gain, axis=1, keepdims=True)
            gains = jnp.where((row_at == n) & (lane_at == i), top, gains)
            node_top = top if node_top is None else jnp.maximum(node_top, top)
        best = jnp.where(row_at == n, node_top, best)
    gain_ref[0] = gains[:NODES, :OWN]

    m1s[...] = best
    copies = []
    for d in range(1, FEAT_AX):
        copies.append(pltpu.make_async_remote_copy(
            src_ref=m1s, dst_ref=m1.at[d], send_sem=m1_send.at[d], recv_sem=m1_recv.at[d],
            device_id={"feat": feat_peer(d)}, device_id_type=MESH))
        copies[-1].start()
    for d, copy in enumerate(copies, 1):
        copy.wait_recv()
        best = jnp.maximum(best, m1[d])
    m2s[...] = best
    for s in range(1, ROWS_AX):
        copies.append(pltpu.make_async_remote_copy(
            src_ref=m2s, dst_ref=m2.at[s], send_sem=m2_send.at[s], recv_sem=m2_recv.at[s],
            device_id={"rows": rows_peer(*ORDER[s])}, device_id_type=MESH))
        copies[-1].start()
    for s, copy in enumerate(copies[FEAT_AX - 1 :], 1):
        copy.wait_recv()
        best = jnp.maximum(best, m2[s])
    row2 = lax.broadcasted_iota(jnp.int32, (1, NODES), 1)
    best_ref[...] = jnp.where(row2 == 0, best[0:1, :NODES], best[1:2, :NODES])

    for copy in copies:
        copy.wait_send()
    for s in range(ROWS_AX):
        if s > 0:
            for copy in first_copies[s]:
                copy.wait_send()
        all_of(rbuf, s, s2_send).wait()
        all_of(rcode, s, c2_send).wait()


def local(features, labels, weights, nodes):
    dma = pltpu.SemaphoreType.DMA
    return pl.pallas_call(
        kernel,
        out_shape=(
            jax.ShapeDtypeStruct((1, NODES, OWN), f32),
            jax.ShapeDtypeStruct((1, NODES), f32),
        ),
        in_specs=[pl.BlockSpec(memory_space=pl.ANY)] + [pl.BlockSpec(memory_space=pltpu.VMEM)] * 3,
        out_specs=(pl.BlockSpec(memory_space=pltpu.VMEM),) * 2,
        scratch_shapes=[
            pltpu.VMEM((512, LOCAL), f32),
            pltpu.VMEM((ROWS_AX, FEAT_AX, 8, 128), bf16),
            pltpu.VMEM((8, 128), bf16),
            pltpu.VMEM((ROWS_AX, FEAT_AX, 8, 128), bf16),
            pltpu.VMEM((ROWS_AX, 8, 128), bf16),
            pltpu.VMEM((ROWS_AX, FEAT_AX, 8, 128), bf16),
            pltpu.VMEM((ROWS_AX, FEAT_AX, 8, 128), bf16),
            pltpu.VMEM((OWN * B, NODES * C), f32),
            pltpu.VMEM((8, 128), f32),
            pltpu.VMEM((FEAT_AX, 8, 128), f32),
            pltpu.VMEM((8, 128), f32),
            pltpu.VMEM((ROWS_AX, 8, 128), f32),
            dma((4,)),
            dma((ROWS_AX,)), dma((ROWS_AX,)), dma((ROWS_AX,)), dma((ROWS_AX,)),
            dma((ROWS_AX,)), dma((ROWS_AX,)), dma((ROWS_AX,)), dma((ROWS_AX,)),
            dma((FEAT_AX,)), dma((FEAT_AX,)), dma((ROWS_AX,)), dma((ROWS_AX,)),
        ],
        compiler_params=pltpu.CompilerParams(collective_id=0, has_side_effects=True, vmem_limit_bytes=48 * 1024 * 1024),
        name="split_scores",
    )(features, labels.reshape(1, -1), weights, nodes)


def solution(mesh):
    return jax.shard_map(
        local,
        mesh=mesh,
        in_specs=(
            P(None, ("rows", "feat")),
            P(("rows", "feat")),
            P("leaf", ("rows", "feat")),
            P("leaf", ("rows", "feat")),
        ),
        out_specs=(P("leaf", None, ("rows", "feat")), P("leaf", None)),
        check_vma=False,
    )
```

```python
import jax
import jax.numpy as jnp
from jax import lax
from jax.experimental import pallas as pl
from jax.experimental.pallas import tpu as pltpu
from jax.sharding import PartitionSpec as P

B = 128
C = 64
NODES = 2
OWN = 4
Z = 8
Y = 2
X = 4
CORES = 2
ROWS_AX = Z * Y
FEAT_AX = X * CORES
LOCAL = 256
GROUP = 2
AHEAD = 2
f32 = jnp.float32
bf16 = jnp.bfloat16
MESH = pl.DeviceIdType.MESH
NT = (((1,), (1,)), ((), ()))
ORDER = [(0, 0), (0, 1), (1, 0), (7, 0), (1, 1), (7, 1), (2, 0), (6, 0), (2, 1), (6, 1), (3, 0), (5, 0), (3, 1), (5, 1), (4, 0), (4, 1)]


def bin_index(x):
    guess = jnp.clip(jnp.ceil(x * (B / 9.0) + (B // 2 - 1)), 0.0, B - 1.0)
    edge_here = (guess + (1.0 - B // 2)) * (9.0 / B)
    edge_before = (guess - (1.0 * (B // 2))) * (9.0 / B)
    up = jnp.where((edge_here < x) & (guess < B - 1.0), 1.0, 0.0)
    down = jnp.where((edge_before >= x) & (guess > 0.0), 1.0, 0.0)
    return guess + up - down


def row_pack(tile, row):
    return jnp.broadcast_to(tile[row : row + 1, :], (16, 128)).astype(bf16)


def mask_tile(tile, bins):
    one, zero = jnp.ones((), bf16), jnp.zeros((), bf16)
    rows = []
    for i in range(OWN):
        halves = []
        for h in range(2):
            packed = row_pack(tile, h * 4 + i)
            halves.append(jnp.where(packed[None] <= bins, one, zero).reshape(B, 128))
        rows.append(jnp.concatenate(halves, axis=1))
    return jnp.concatenate(rows, axis=0)


def target_tile(tile, classes):
    zero = jnp.zeros((), bf16)
    parts = [[], []]
    for h in range(2):
        hit = row_pack(tile, h * 4)[None] == classes
        for n in range(NODES):
            weight = jnp.broadcast_to(row_pack(tile, h * 4 + 1 + n)[None], hit.shape)
            parts[n].append(jnp.where(hit, weight, zero).reshape(C, 128))
    return jnp.concatenate([jnp.concatenate(p, axis=1) for p in parts], axis=0)


def ratio(values):
    return jnp.sum(values * values, axis=0, keepdims=True) / jnp.maximum(jnp.sum(values, axis=0, keepdims=True), 1.0)


def kernel(
    feat_hbm, lab_hbm, wei_hbm, node_hbm, out_ref,
    feat_v, lab_v, wei_v, node_v, send, zbuf, rbuf, acc, m1s, m1, m2s, m2,
    in_sem, s1_send, s1_recv, s2_send, s2_recv, m1_send, m1_recv, m2_send, m2_recv,
):
    my_rows, my_feat = lax.axis_index("rows"), lax.axis_index("feat")
    z, y = lax.div(my_rows, Y), lax.rem(my_rows, Y)

    def rows_peer(dz, dy):
        return lax.rem(z + dz, Z) * Y + lax.rem(y + dy, Y)

    def feat_peer(d):
        return lax.rem(my_feat + d, FEAT_AX)

    barrier = pltpu.get_barrier_semaphore()
    for dz, dy in reversed(ORDER[1:]):
        pl.semaphore_signal(barrier, inc=1, device_id={"rows": rows_peer(dz, dy)}, device_id_type=MESH)
    for d in range(1, FEAT_AX):
        pl.semaphore_signal(barrier, inc=1, device_id={"feat": feat_peer(d)}, device_id_type=MESH)

    loads = [
        pltpu.make_async_copy(feat_hbm, feat_v, in_sem.at[0]),
        pltpu.make_async_copy(lab_hbm, lab_v, in_sem.at[1]),
        pltpu.make_async_copy(wei_hbm, wei_v, in_sem.at[2]),
        pltpu.make_async_copy(node_hbm, node_v, in_sem.at[3]),
    ]
    for load in loads:
        load.start()
    for load in loads:
        load.wait()

    label = lab_v[...].astype(f32)
    weight = wei_v[...].astype(f32)
    node = node_v[...]
    w0 = jnp.where(node == 0, weight, 0.0)
    w1 = jnp.where(node == 1, weight, 0.0)
    pad = jnp.zeros_like(w0)
    lines = []
    for h in range(2):
        cut = slice(h * 128, (h + 1) * 128)
        lines += [label[:, cut], w0[:, cut], w1[:, cut], pad[:, cut]]
    codes = jnp.concatenate(lines, axis=0).astype(bf16)
    sub = lax.broadcasted_iota(jnp.int32, (4, 8, 128), 1)

    def binned(r):
        values = bin_index(feat_v[pl.ds(pl.multiple_of(r * 32, 32), 32), :])
        a = values[:, :128].reshape(4, 8, 128)
        b = values[:, 128:].reshape(4, 8, 128)
        first = jnp.where(sub < 4, a, pltpu.roll(b, 4, 1))
        second = jnp.where(sub < 4, pltpu.roll(a, 4, 1), b)
        return jnp.stack([first, second], axis=1).reshape(8, 8, 128).astype(bf16)

    def place(r, carry):
        send[r, :FEAT_AX] = binned(r)
        send[r, FEAT_AX] = codes
        return carry

    lax.fori_loop(0, ROWS_AX, place, 0)
    zbuf[0, :FEAT_AX] = binned(my_rows)
    zbuf[0, FEAT_AX] = codes
    acc[...] = jnp.zeros_like(acc)

    pl.semaphore_wait(barrier, ROWS_AX - 1 + FEAT_AX - 1)

    for s in range(1, ROWS_AX):
        peer = rows_peer(*ORDER[s])
        pltpu.make_async_remote_copy(
            src_ref=send.at[peer], dst_ref=zbuf.at[s], send_sem=s1_send, recv_sem=s1_recv.at[s],
            device_id={"rows": peer}, device_id_type=MESH).start()

    def forward(s, wait=True):
        if wait:
            pltpu.make_async_copy(zbuf.at[s], zbuf.at[s], s1_recv.at[s]).wait()
        for d in range(1, FEAT_AX):
            peer = feat_peer(d)
            for part, block in ((0, peer), (1, FEAT_AX)):
                pltpu.make_async_remote_copy(
                    src_ref=zbuf.at[s, block], dst_ref=rbuf.at[s, d, part], send_sem=s2_send, recv_sem=s2_recv.at[s],
                    device_id={"feat": peer}, device_id_type=MESH).start()

    bins = (lax.broadcasted_iota(jnp.int32, (8, 16, 128), 0) * 16 + lax.broadcasted_iota(jnp.int32, (8, 16, 128), 1)).astype(f32).astype(bf16)
    classes = bins[: C // 16]

    def use(g):
        masks, targets = [], []
        for u in range(GROUP):
            part = rbuf.at[g * GROUP + u, pl.ds(1, FEAT_AX - 1)]
            pltpu.make_async_copy(part, part, s2_recv.at[g * GROUP + u]).wait()
        for u in range(GROUP):
            s = g * GROUP + u
            masks.append(mask_tile(zbuf[s, my_feat].astype(f32), bins))
            targets.append(target_tile(zbuf[s, FEAT_AX].astype(f32), classes))
            for d in range(1, FEAT_AX):
                masks.append(mask_tile(rbuf[s, d, 0].astype(f32), bins))
                targets.append(target_tile(rbuf[s, d, 1].astype(f32), classes))
        acc[...] += lax.dot_general(jnp.concatenate(masks, axis=1), jnp.concatenate(targets, axis=1), NT, preferred_element_type=f32)

    forward(0, wait=False)
    for s in range(1, AHEAD * GROUP):
        forward(s)

    def step(g, carry):
        for u in range(GROUP):
            forward((g + AHEAD) * GROUP + u)
        use(g)
        return carry

    def tail(g, carry):
        use(g)
        return carry

    steps = ROWS_AX // GROUP
    lax.fori_loop(0, steps - AHEAD, step, 0)
    lax.fori_loop(steps - AHEAD, steps, tail, 0)

    row_at = lax.broadcasted_iota(jnp.int32, (8, 128), 0)
    lane_at = lax.broadcasted_iota(jnp.int32, (8, 128), 1)
    gains = jnp.zeros((8, 128), f32)
    best = jnp.zeros((8, 128), f32)
    for n in range(NODES):
        node_top = None
        for i in range(OWN):
            left = acc[i * B : (i + 1) * B, :].T[n * C : (n + 1) * C, :]
            total = left[:, B - 1 : B]
            right = total - left
            gain = ratio(left) + ratio(right) - ratio(total)
            top = jnp.max(gain, axis=1, keepdims=True)
            gains = jnp.where((row_at == n) & (lane_at == i), top, gains)
            node_top = top if node_top is None else jnp.maximum(node_top, top)
        best = jnp.where(row_at == n, node_top, best)

    m1s[...] = best
    for d in range(1, FEAT_AX):
        pltpu.make_async_remote_copy(
            src_ref=m1s, dst_ref=m1.at[d], send_sem=m1_send, recv_sem=m1_recv,
            device_id={"feat": feat_peer(d)}, device_id_type=MESH).start()
    m1_all, m2_all = m1.at[pl.ds(1, FEAT_AX - 1)], m2.at[pl.ds(1, ROWS_AX - 1)]
    pltpu.make_async_copy(m1_all, m1_all, m1_recv).wait()
    best = jnp.maximum(best, jnp.max(m1[1:], axis=0))
    m2s[...] = best
    for s in range(1, ROWS_AX):
        pltpu.make_async_remote_copy(
            src_ref=m2s, dst_ref=m2.at[s], send_sem=m2_send, recv_sem=m2_recv,
            device_id={"rows": rows_peer(*ORDER[s])}, device_id_type=MESH).start()
    z_all, r_all = zbuf.at[pl.ds(1, ROWS_AX - 1)], rbuf.at[:, pl.ds(1, FEAT_AX - 1)]
    pltpu.make_async_copy(z_all, z_all, s1_send).wait()
    pltpu.make_async_copy(r_all, r_all, s2_send).wait()
    pltpu.make_async_copy(m1_all, m1_all, m1_send).wait()
    pltpu.make_async_copy(m2_all, m2_all, m2_send).wait()
    pltpu.make_async_copy(m2_all, m2_all, m2_recv).wait()
    best = jnp.maximum(best, jnp.max(m2[1:], axis=0))
    out_ref[...] = jnp.where(lane_at < OWN, gains, best)


def local(features, labels, weights, nodes):
    dma = pltpu.SemaphoreType.DMA
    result = pl.pallas_call(
        kernel,
        out_shape=jax.ShapeDtypeStruct((8, 128), f32),
        in_specs=[pl.BlockSpec(memory_space=pl.ANY)] * 4,
        out_specs=pl.BlockSpec(memory_space=pltpu.VMEM),
        scratch_shapes=[
            pltpu.VMEM((512, LOCAL), f32),
            pltpu.VMEM((1, LOCAL), jnp.int32),
            pltpu.VMEM((1, LOCAL), bf16),
            pltpu.VMEM((1, LOCAL), jnp.int32),
            pltpu.VMEM((ROWS_AX, FEAT_AX + 1, 8, 128), bf16),
            pltpu.VMEM((ROWS_AX, FEAT_AX + 1, 8, 128), bf16),
            pltpu.VMEM((ROWS_AX, FEAT_AX, 2, 8, 128), bf16),
            pltpu.VMEM((OWN * B, NODES * C), f32),
            pltpu.VMEM((8, 128), f32),
            pltpu.VMEM((FEAT_AX, 8, 128), f32),
            pltpu.VMEM((8, 128), f32),
            pltpu.VMEM((ROWS_AX, 8, 128), f32),
            dma((4,)), dma(()), dma((ROWS_AX,)), dma(()), dma((ROWS_AX,)), dma(()), dma(()), dma(()), dma(()),
        ],
        compiler_params=pltpu.CompilerParams(collective_id=0, has_side_effects=True, vmem_limit_bytes=67043328),
        name="split_scores",
    )(features, labels.reshape(1, -1), weights, nodes)
    return result[None, :NODES, :OWN], result[:NODES, OWN][None]


def solution(mesh):
    return jax.shard_map(
        local,
        mesh=mesh,
        in_specs=(
            P(None, ("rows", "feat")),
            P(("rows", "feat")),
            P("leaf", ("rows", "feat")),
            P("leaf", ("rows", "feat")),
        ),
        out_specs=(P("leaf", None, ("rows", "feat")), P("leaf", None)),
        check_vma=False,
    )
```

```python
import jax
import jax.numpy as jnp
from jax import lax
from jax.experimental import pallas as pl
from jax.experimental.pallas import tpu as pltpu
from jax.sharding import PartitionSpec as P

B = 128
C = 64
NODES = 2
OWN = 4
Z = 8
Y = 2
X = 4
CORES = 2
ROWS_AX = Z * Y
FEAT_AX = X * CORES
LOCAL = 256
GROUP = 2
AHEAD = 3
f32 = jnp.float32
bf16 = jnp.bfloat16
MESH = pl.DeviceIdType.MESH
NT = (((1,), (1,)), ((), ()))
ORDER = [(0, 0), (0, 1), (1, 0), (7, 0), (1, 1), (7, 1), (2, 0), (6, 0), (2, 1), (6, 1), (3, 0), (5, 0), (3, 1), (5, 1), (4, 0), (4, 1)]
LEVELS = [(1, 4), (4, 8), (8, 12), (12, 15), (15, 16)]


def bin_index(x):
    guess = jnp.clip(jnp.ceil(x * (B / 9.0) + (B // 2 - 1)), 0.0, B - 1.0)
    edge_here = (guess + (1.0 - B // 2)) * (9.0 / B)
    edge_before = (guess - (1.0 * (B // 2))) * (9.0 / B)
    up = jnp.where((edge_here < x) & (guess < B - 1.0), 1.0, 0.0)
    down = jnp.where((edge_before >= x) & (guess > 0.0), 1.0, 0.0)
    return guess + up - down


def row_pack(tile, row):
    return jnp.broadcast_to(tile[row : row + 1, :], (16, 128)).astype(bf16)


def mask_tile(tile, bins):
    one, zero = jnp.ones((), bf16), jnp.zeros((), bf16)
    rows = []
    for i in range(OWN):
        halves = []
        for h in range(2):
            packed = row_pack(tile, h * 4 + i)
            halves.append(jnp.where(packed[None] <= bins, one, zero).reshape(B, 128))
        rows.append(jnp.concatenate(halves, axis=1))
    return jnp.concatenate(rows, axis=0)


def target_tile(tile, classes):
    zero = jnp.zeros((), bf16)
    parts = [[], []]
    for h in range(2):
        hit = row_pack(tile, h * 4)[None] == classes
        for n in range(NODES):
            weight = jnp.broadcast_to(row_pack(tile, h * 4 + 1 + n)[None], hit.shape)
            parts[n].append(jnp.where(hit, weight, zero).reshape(C, 128))
    return jnp.concatenate([jnp.concatenate(p, axis=1) for p in parts], axis=0)


def ratio(values):
    return jnp.sum(values * values, axis=0, keepdims=True) / jnp.maximum(jnp.sum(values, axis=0, keepdims=True), 1.0)


def kernel(
    feat_hbm, lab_hbm, wei_hbm, node_hbm, out_ref,
    feat_v, lab_v, wei_v, node_v, send, zbuf, rbuf, acc, m1s, m1, m2s, m2,
    relay, in_sem, s1_send, s1_recv, s2_send, s2_recv, m1_send, m1_recv, m2_send, m2_recv,
):
    my_rows, my_feat = lax.axis_index("rows"), lax.axis_index("feat")
    z, y = lax.div(my_rows, Y), lax.rem(my_rows, Y)

    def rows_peer(dz, dy):
        return lax.rem(z + dz, Z) * Y + lax.rem(y + dy, Y)

    def feat_peer(d):
        return lax.rem(my_feat + d, FEAT_AX)

    barrier = pltpu.get_barrier_semaphore()
    for dz, dy in ORDER[slice(*LEVELS[0])]:
        pl.semaphore_signal(barrier, inc=1, device_id={"rows": rows_peer(dz, dy)}, device_id_type=MESH)
    for d in range(1, FEAT_AX):
        pl.semaphore_signal(barrier, inc=1, device_id={"feat": feat_peer(d)}, device_id_type=MESH)

    loads = [
        pltpu.make_async_copy(feat_hbm, feat_v, in_sem.at[0]),
        pltpu.make_async_copy(lab_hbm, lab_v, in_sem.at[1]),
        pltpu.make_async_copy(wei_hbm, wei_v, in_sem.at[2]),
        pltpu.make_async_copy(node_hbm, node_v, in_sem.at[3]),
    ]
    for load in loads:
        load.start()
    for load in loads:
        load.wait()

    label = lab_v[...].astype(f32)
    weight = wei_v[...].astype(f32)
    node = node_v[...]
    w0 = jnp.where(node == 0, weight, 0.0)
    w1 = jnp.where(node == 1, weight, 0.0)
    pad = jnp.zeros_like(w0)
    lines = []
    for h in range(2):
        cut = slice(h * 128, (h + 1) * 128)
        lines += [label[:, cut], w0[:, cut], w1[:, cut], pad[:, cut]]
    codes = jnp.concatenate(lines, axis=0).astype(bf16)
    sub = lax.broadcasted_iota(jnp.int32, (4, 8, 128), 1)

    def binned(r):
        values = bin_index(feat_v[pl.ds(pl.multiple_of(r * 32, 32), 32), :])
        a = values[:, :128].reshape(4, 8, 128)
        b = values[:, 128:].reshape(4, 8, 128)
        first = jnp.where(sub < 4, a, pltpu.roll(b, 4, 1))
        second = jnp.where(sub < 4, pltpu.roll(a, 4, 1), b)
        return jnp.stack([first, second], axis=1).reshape(8, 8, 128).astype(bf16)

    def place(r, carry):
        send[r, :FEAT_AX] = binned(r)
        send[r, FEAT_AX] = codes
        return carry

    lax.fori_loop(0, ROWS_AX, place, 0)
    zbuf[0, :FEAT_AX] = binned(my_rows)
    zbuf[0, FEAT_AX] = codes
    acc[...] = jnp.zeros_like(acc)

    def forward(s, wait=True):
        if wait:
            pltpu.make_async_copy(zbuf.at[s], zbuf.at[s], s1_recv.at[s]).wait()
        for d in range(1, FEAT_AX):
            peer = feat_peer(d)
            for part, block in ((0, peer), (1, FEAT_AX)):
                pltpu.make_async_remote_copy(
                    src_ref=zbuf.at[s, block], dst_ref=rbuf.at[s, d, part], send_sem=s2_send, recv_sem=s2_recv.at[s],
                    device_id={"feat": peer}, device_id_type=MESH).start()

    bins = (lax.broadcasted_iota(jnp.int32, (8, 16, 128), 0) * 16 + lax.broadcasted_iota(jnp.int32, (8, 16, 128), 1)).astype(f32).astype(bf16)
    classes = bins[: C // 16]

    def use(g):
        masks, targets = [], []
        for u in range(GROUP):
            part = rbuf.at[g * GROUP + u, pl.ds(1, FEAT_AX - 1)]
            pltpu.make_async_copy(part, part, s2_recv.at[g * GROUP + u]).wait()
        for u in range(GROUP):
            s = g * GROUP + u
            masks.append(mask_tile(zbuf[s, my_feat].astype(f32), bins))
            targets.append(target_tile(zbuf[s, FEAT_AX].astype(f32), classes))
            for d in range(1, FEAT_AX):
                masks.append(mask_tile(rbuf[s, d, 0].astype(f32), bins))
                targets.append(target_tile(rbuf[s, d, 1].astype(f32), classes))
        acc[...] += lax.dot_general(jnp.concatenate(masks, axis=1), jnp.concatenate(targets, axis=1), NT, preferred_element_type=f32)

    def send_level(k):
        for s in range(*LEVELS[k]):
            peer = rows_peer(*ORDER[s])
            pltpu.make_async_remote_copy(
                src_ref=send.at[peer], dst_ref=zbuf.at[s], send_sem=s1_send, recv_sem=s1_recv.at[s],
                device_id={"rows": peer}, device_id_type=MESH).start()

    pl.semaphore_wait(barrier, LEVELS[0][1] - LEVELS[0][0] + FEAT_AX - 1)
    for k in range(len(LEVELS)):
        if k > 0:
            for side in range(2):
                pl.semaphore_wait(relay.at[k - 1, side], 1)
        if k + 1 < len(LEVELS):
            for side, dz in enumerate((1, Z - 1)):
                pl.semaphore_signal(relay.at[k, side], inc=1, device_id={"rows": rows_peer(dz, 0)}, device_id_type=MESH)
        send_level(k)
        if k == 0:
            forward(0, wait=False)
    for s in range(1, AHEAD * GROUP):
        forward(s)

    def step(g, carry):
        for u in range(GROUP):
            forward((g + AHEAD) * GROUP + u)
        use(g)
        return carry

    def tail(g, carry):
        use(g)
        return carry

    steps = ROWS_AX // GROUP
    lax.fori_loop(0, steps - AHEAD, step, 0)
    lax.fori_loop(steps - AHEAD, steps, tail, 0)

    row_at = lax.broadcasted_iota(jnp.int32, (8, 128), 0)
    lane_at = lax.broadcasted_iota(jnp.int32, (8, 128), 1)
    gains = jnp.zeros((8, 128), f32)
    best = jnp.zeros((8, 128), f32)
    for n in range(NODES):
        node_top = None
        for i in range(OWN):
            left = acc[i * B : (i + 1) * B, :].T[n * C : (n + 1) * C, :]
            total = left[:, B - 1 : B]
            right = total - left
            gain = ratio(left) + ratio(right) - ratio(total)
            top = jnp.max(gain, axis=1, keepdims=True)
            gains = jnp.where((row_at == n) & (lane_at == i), top, gains)
            node_top = top if node_top is None else jnp.maximum(node_top, top)
        best = jnp.where(row_at == n, node_top, best)

    m1s[...] = best
    for d in range(1, FEAT_AX):
        pltpu.make_async_remote_copy(
            src_ref=m1s, dst_ref=m1.at[d], send_sem=m1_send, recv_sem=m1_recv,
            device_id={"feat": feat_peer(d)}, device_id_type=MESH).start()
    m1_all, m2_all = m1.at[pl.ds(1, FEAT_AX - 1)], m2.at[pl.ds(1, ROWS_AX - 1)]
    pltpu.make_async_copy(m1_all, m1_all, m1_recv).wait()
    best = jnp.maximum(best, jnp.max(m1[1:], axis=0))
    m2s[...] = best
    for s in range(1, ROWS_AX):
        pltpu.make_async_remote_copy(
            src_ref=m2s, dst_ref=m2.at[s], send_sem=m2_send, recv_sem=m2_recv,
            device_id={"rows": rows_peer(*ORDER[s])}, device_id_type=MESH).start()
    z_all, r_all = zbuf.at[pl.ds(1, ROWS_AX - 1)], rbuf.at[:, pl.ds(1, FEAT_AX - 1)]
    pltpu.make_async_copy(z_all, z_all, s1_send).wait()
    pltpu.make_async_copy(r_all, r_all, s2_send).wait()
    pltpu.make_async_copy(m1_all, m1_all, m1_send).wait()
    pltpu.make_async_copy(m2_all, m2_all, m2_send).wait()
    pltpu.make_async_copy(m2_all, m2_all, m2_recv).wait()
    best = jnp.maximum(best, jnp.max(m2[1:], axis=0))
    out_ref[...] = jnp.where(lane_at < OWN, gains, best)


def local(features, labels, weights, nodes):
    dma = pltpu.SemaphoreType.DMA
    result = pl.pallas_call(
        kernel,
        out_shape=jax.ShapeDtypeStruct((8, 128), f32),
        in_specs=[pl.BlockSpec(memory_space=pl.ANY)] * 4,
        out_specs=pl.BlockSpec(memory_space=pltpu.VMEM),
        scratch_shapes=[
            pltpu.VMEM((512, LOCAL), f32),
            pltpu.VMEM((1, LOCAL), jnp.int32),
            pltpu.VMEM((1, LOCAL), bf16),
            pltpu.VMEM((1, LOCAL), jnp.int32),
            pltpu.VMEM((ROWS_AX, FEAT_AX + 1, 8, 128), bf16),
            pltpu.VMEM((ROWS_AX, FEAT_AX + 1, 8, 128), bf16),
            pltpu.VMEM((ROWS_AX, FEAT_AX, 2, 8, 128), bf16),
            pltpu.VMEM((OWN * B, NODES * C), f32),
            pltpu.VMEM((8, 128), f32),
            pltpu.VMEM((FEAT_AX, 8, 128), f32),
            pltpu.VMEM((8, 128), f32),
            pltpu.VMEM((ROWS_AX, 8, 128), f32),
            pltpu.SemaphoreType.REGULAR((len(LEVELS) - 1, 2)),
            dma((4,)), dma(()), dma((ROWS_AX,)), dma(()), dma((ROWS_AX,)), dma(()), dma(()), dma(()), dma(()),
        ],
        compiler_params=pltpu.CompilerParams(collective_id=0, has_side_effects=True, vmem_limit_bytes=48 * 1024 * 1024),
        name="split_scores",
    )(*[pltpu.with_memory_space_constraint(v, pltpu.HBM) for v in (features, labels.reshape(1, -1), weights, nodes)])
    return result[None, :NODES, :OWN], result[:NODES, OWN][None]


def solution(mesh):
    return jax.shard_map(
        local,
        mesh=mesh,
        in_specs=(
            P(None, ("rows", "feat")),
            P(("rows", "feat")),
            P("leaf", ("rows", "feat")),
            P("leaf", ("rows", "feat")),
        ),
        out_specs=(P("leaf", None, ("rows", "feat")), P("leaf", None)),
        check_vma=False,
    )
```

```python
import jax
import jax.numpy as jnp
from jax import lax
from jax.experimental import pallas as pl
from jax.experimental.pallas import tpu as pltpu
from jax.sharding import PartitionSpec as P

B = 128
C = 64
NODES = 2
OWN = 4
Z = 8
Y = 2
X = 4
CORES = 2
ROWS_AX = Z * Y
CHUNKS = 4
FEAT_AX = X * CORES
LOCAL = 256
f32 = jnp.float32
bf16 = jnp.bfloat16
MESH = pl.DeviceIdType.MESH
NT = (((1,), (1,)), ((), ()))
ORDER = [(0, 0), (0, 1), (1, 0), (7, 0), (1, 1), (7, 1), (2, 0), (6, 0), (2, 1), (6, 1), (3, 0), (5, 0), (3, 1), (5, 1), (4, 0), (4, 1)]
LEVELS = [(1, 4), (4, 8), (8, 12), (12, 15), (15, 16)]


def bin_index(x):
    guess = jnp.clip(jnp.ceil(x * (B / 9.0) + (B // 2 - 1)), 0.0, B - 1.0)
    edge_here = (guess + (1.0 - B // 2)) * (9.0 / B)
    edge_before = (guess - (1.0 * (B // 2))) * (9.0 / B)
    up = jnp.where((edge_here < x) & (guess < B - 1.0), 1.0, 0.0)
    down = jnp.where((edge_before >= x) & (guess > 0.0), 1.0, 0.0)
    return guess + up - down


def row_pack(tile, row):
    return jnp.broadcast_to(tile[row : row + 1, :], (16, 128)).astype(bf16)


def mask_tile(tile, bins):
    one, zero = jnp.ones((), bf16), jnp.zeros((), bf16)
    rows = []
    for i in range(OWN):
        halves = []
        for h in range(2):
            packed = row_pack(tile, h * 4 + i)
            halves.append(jnp.where(packed[None] <= bins, one, zero).reshape(B, 128))
        rows.append(jnp.concatenate(halves, axis=1))
    return jnp.concatenate(rows, axis=0)


def target_tile(tile, classes):
    zero = jnp.zeros((), bf16)
    parts = [[], []]
    for h in range(2):
        hit = row_pack(tile, h * 4)[None] == classes
        for n in range(NODES):
            weight = jnp.broadcast_to(row_pack(tile, h * 4 + 1 + n)[None], hit.shape)
            parts[n].append(jnp.where(hit, weight, zero).reshape(C, 128))
    return jnp.concatenate([jnp.concatenate(p, axis=1) for p in parts], axis=0)


def ratio(values):
    return jnp.sum(values * values, axis=0, keepdims=True) / jnp.maximum(jnp.sum(values, axis=0, keepdims=True), 1.0)


def kernel(
    feat_hbm, lab_hbm, wei_hbm, node_hbm, out_ref,
    feat_v, lab_v, wei_v, node_v, send, zbuf, rbuf, acc, m1s, m1, m2s, m2,
    relay, in_sem, s1_send, s1_recv, s2_send, s2_recv, m1_send, m1_recv, m2_send, m2_recv,
):
    my_rows, my_feat = lax.axis_index("rows"), lax.axis_index("feat")
    z, y = lax.div(my_rows, Y), lax.rem(my_rows, Y)

    def rows_peer(dz, dy):
        return lax.rem(z + dz, Z) * Y + lax.rem(y + dy, Y)

    def feat_peer(d):
        return lax.rem(my_feat + d, FEAT_AX)

    barrier = pltpu.get_barrier_semaphore()
    for dz, dy in ORDER[slice(*LEVELS[0])]:
        pl.semaphore_signal(barrier, inc=1, device_id={"rows": rows_peer(dz, dy)}, device_id_type=MESH)
    for d in range(1, FEAT_AX):
        pl.semaphore_signal(barrier, inc=1, device_id={"feat": feat_peer(d)}, device_id_type=MESH)

    loads = [
        pltpu.make_async_copy(lab_hbm, lab_v, in_sem.at[CHUNKS]),
        pltpu.make_async_copy(wei_hbm, wei_v, in_sem.at[CHUNKS + 1]),
        pltpu.make_async_copy(node_hbm, node_v, in_sem.at[CHUNKS + 2]),
    ]
    chunk_loads = []
    for q in range(CHUNKS):
        part = pl.ds(q * (512 // CHUNKS), 512 // CHUNKS)
        chunk_loads.append(pltpu.make_async_copy(feat_hbm.at[part], feat_v.at[part], in_sem.at[q]))
    for load in loads + chunk_loads:
        load.start()
    for load in loads:
        load.wait()

    label = lab_v[...].astype(f32)
    weight = wei_v[...].astype(f32)
    node = node_v[...]
    w0 = jnp.where(node == 0, weight, 0.0)
    w1 = jnp.where(node == 1, weight, 0.0)
    pad = jnp.zeros_like(w0)
    lines = []
    for h in range(2):
        cut = slice(h * 128, (h + 1) * 128)
        lines += [label[:, cut], w0[:, cut], w1[:, cut], pad[:, cut]]
    codes = jnp.concatenate(lines, axis=0).astype(bf16)
    sub = lax.broadcasted_iota(jnp.int32, (4, 8, 128), 1)

    def binned(r):
        values = bin_index(feat_v[pl.ds(pl.multiple_of(r * 32, 32), 32), :])
        a = values[:, :128].reshape(4, 8, 128)
        b = values[:, 128:].reshape(4, 8, 128)
        first = jnp.where(sub < 4, a, pltpu.roll(b, 4, 1))
        second = jnp.where(sub < 4, pltpu.roll(a, 4, 1), b)
        return jnp.stack([first, second], axis=1).reshape(8, 8, 128).astype(bf16)

    def place(r, carry):
        send[r, :FEAT_AX] = binned(r)
        send[r, FEAT_AX] = codes
        return carry

    for q in range(CHUNKS):
        chunk_loads[q].wait()
        lax.fori_loop(q * (ROWS_AX // CHUNKS), (q + 1) * (ROWS_AX // CHUNKS), place, 0)
    zbuf[0, :FEAT_AX] = binned(my_rows)
    zbuf[0, FEAT_AX] = codes
    acc[...] = jnp.zeros_like(acc)

    def forward(s, wait=True):
        if wait:
            pltpu.make_async_copy(zbuf.at[s], zbuf.at[s], s1_recv.at[s]).wait()
        for d in range(1, FEAT_AX):
            peer = feat_peer(d)
            for part, block in ((0, peer), (1, FEAT_AX)):
                pltpu.make_async_remote_copy(
                    src_ref=zbuf.at[s, block], dst_ref=rbuf.at[s, d, part], send_sem=s2_send, recv_sem=s2_recv.at[s],
                    device_id={"feat": peer}, device_id_type=MESH).start()

    bins = (lax.broadcasted_iota(jnp.int32, (8, 16, 128), 0) * 16 + lax.broadcasted_iota(jnp.int32, (8, 16, 128), 1)).astype(f32).astype(bf16)
    classes = bins[: C // 16]

    def use(start, count):
        masks, targets = [], []
        for u in range(count):
            part = rbuf.at[start + u, pl.ds(1, FEAT_AX - 1)]
            pltpu.make_async_copy(part, part, s2_recv.at[start + u]).wait()
        for u in range(count):
            s = start + u
            masks.append(mask_tile(zbuf[s, my_feat].astype(f32), bins))
            targets.append(target_tile(zbuf[s, FEAT_AX].astype(f32), classes))
            for d in range(1, FEAT_AX):
                masks.append(mask_tile(rbuf[s, d, 0].astype(f32), bins))
                targets.append(target_tile(rbuf[s, d, 1].astype(f32), classes))
        acc[...] += lax.dot_general(jnp.concatenate(masks, axis=1), jnp.concatenate(targets, axis=1), NT, preferred_element_type=f32)

    def send_level(k):
        for s in range(*LEVELS[k]):
            peer = rows_peer(*ORDER[s])
            pltpu.make_async_remote_copy(
                src_ref=send.at[peer], dst_ref=zbuf.at[s], send_sem=s1_send, recv_sem=s1_recv.at[s],
                device_id={"rows": peer}, device_id_type=MESH).start()

    def level(k):
        if k > 0:
            for side in range(2):
                pl.semaphore_wait(relay.at[k - 1, side], 1)
        if k + 1 < len(LEVELS):
            for side, dz in enumerate((1, Z - 1)):
                pl.semaphore_signal(relay.at[k, side], inc=1, device_id={"rows": rows_peer(dz, 0)}, device_id_type=MESH)
        send_level(k)

    def forward_all(first, last):
        for s in range(first, last):
            forward(s, wait=s > 0)

    pl.semaphore_wait(barrier, LEVELS[0][1] - LEVELS[0][0] + FEAT_AX - 1)
    level(0)
    forward_all(0, 1)
    level(1)
    forward_all(1, 4)
    level(2)
    use(0, 1)
    level(3)
    forward_all(4, 8)

    def step(g, carry):
        @pl.when(g == 1)
        def _():
            level(4)
            forward_all(8, 12)

        @pl.when(g == 2)
        def _():
            forward_all(12, 15)

        @pl.when(g == 3)
        def _():
            forward_all(15, 16)

        use(1 + 2 * g, 2)
        return carry

    lax.fori_loop(0, 7, step, 0)
    use(15, 1)

    row_at = lax.broadcasted_iota(jnp.int32, (8, 128), 0)
    lane_at = lax.broadcasted_iota(jnp.int32, (8, 128), 1)
    gains = jnp.zeros((8, 128), f32)
    best = jnp.zeros((1, 128), f32)
    lane_row = lax.broadcasted_iota(jnp.int32, (1, 128), 1)
    for n in range(NODES):
        node_top = None
        for i in range(OWN):
            left = acc[i * B : (i + 1) * B, :].T[n * C : (n + 1) * C, :]
            total = left[:, B - 1 : B]
            right = total - left
            gain = ratio(left) + ratio(right) - ratio(total)
            top = jnp.max(gain, axis=1, keepdims=True)
            gains = jnp.where((row_at == n) & (lane_at == i), top, gains)
            node_top = top if node_top is None else jnp.maximum(node_top, top)
        best = jnp.where(lane_row == n, node_top, best)

    m1s[...] = best
    for d in range(1, FEAT_AX):
        pltpu.make_async_remote_copy(
            src_ref=m1s, dst_ref=m1.at[d], send_sem=m1_send, recv_sem=m1_recv,
            device_id={"feat": feat_peer(d)}, device_id_type=MESH).start()
    m1_all, m2_all = m1.at[pl.ds(1, FEAT_AX - 1)], m2.at[pl.ds(1, ROWS_AX - 1)]
    pltpu.make_async_copy(m1_all, m1_all, m1_recv).wait()
    best = jnp.maximum(best, jnp.max(m1[1:], axis=0))
    m2s[...] = best
    for s in range(1, ROWS_AX):
        pltpu.make_async_remote_copy(
            src_ref=m2s, dst_ref=m2.at[s], send_sem=m2_send, recv_sem=m2_recv,
            device_id={"rows": rows_peer(*ORDER[s])}, device_id_type=MESH).start()
    z_all, r_all = zbuf.at[pl.ds(1, ROWS_AX - 1)], rbuf.at[:, pl.ds(1, FEAT_AX - 1)]
    pltpu.make_async_copy(z_all, z_all, s1_send).wait()
    pltpu.make_async_copy(r_all, r_all, s2_send).wait()
    pltpu.make_async_copy(m1_all, m1_all, m1_send).wait()
    pltpu.make_async_copy(m2_all, m2_all, m2_send).wait()
    pltpu.make_async_copy(m2_all, m2_all, m2_recv).wait()
    best = jnp.maximum(best, jnp.max(m2[1:], axis=0))
    best_column = jnp.where(row_at == 0, best[:, 0:1], best[:, 1:2])
    out_ref[...] = jnp.where(lane_at < OWN, gains, best_column)


def local(features, labels, weights, nodes):
    dma = pltpu.SemaphoreType.DMA
    result = pl.pallas_call(
        kernel,
        out_shape=jax.ShapeDtypeStruct((8, 128), f32),
        in_specs=[pl.BlockSpec(memory_space=pl.ANY)] * 4,
        out_specs=pl.BlockSpec(memory_space=pltpu.VMEM),
        scratch_shapes=[
            pltpu.VMEM((512, LOCAL), f32),
            pltpu.VMEM((1, LOCAL), jnp.int32),
            pltpu.VMEM((1, LOCAL), bf16),
            pltpu.VMEM((1, LOCAL), jnp.int32),
            pltpu.VMEM((ROWS_AX, FEAT_AX + 1, 8, 128), bf16),
            pltpu.VMEM((ROWS_AX, FEAT_AX + 1, 8, 128), bf16),
            pltpu.VMEM((ROWS_AX, FEAT_AX, 2, 8, 128), bf16),
            pltpu.VMEM((OWN * B, NODES * C), f32),
            pltpu.VMEM((1, 128), f32),
            pltpu.VMEM((FEAT_AX, 1, 128), f32),
            pltpu.VMEM((1, 128), f32),
            pltpu.VMEM((ROWS_AX, 1, 128), f32),
            pltpu.SemaphoreType.REGULAR((len(LEVELS) - 1, 2)),
            dma((CHUNKS + 3,)), dma(()), dma((ROWS_AX,)), dma(()), dma((ROWS_AX,)), dma(()), dma(()), dma(()), dma(()),
        ],
        compiler_params=pltpu.CompilerParams(collective_id=0, has_side_effects=True, vmem_limit_bytes=48 * 1024 * 1024),
        name="split_scores",
    )(*[pltpu.with_memory_space_constraint(v, pltpu.HBM) for v in (features, labels.reshape(1, -1), weights, nodes)])
    return result[None, :NODES, :OWN], result[:NODES, OWN][None]


def solution(mesh):
    return jax.shard_map(
        local,
        mesh=mesh,
        in_specs=(
            P(None, ("rows", "feat")),
            P(("rows", "feat")),
            P("leaf", ("rows", "feat")),
            P("leaf", ("rows", "feat")),
        ),
        out_specs=(P("leaf", None, ("rows", "feat")), P("leaf", None)),
        check_vma=False,
    )
```

```python
import jax
import jax.numpy as jnp
from jax import lax
from jax.experimental import pallas as pl
from jax.experimental.pallas import tpu as pltpu
from jax.sharding import PartitionSpec as P

B = 128
C = 64
NODES = 2
OWN = 4
Z = 8
Y = 2
X = 4
CORES = 2
ROWS_AX = Z * Y
CHUNKS = 4
FEAT_AX = X * CORES
LOCAL = 256
f32 = jnp.float32
bf16 = jnp.bfloat16
MESH = pl.DeviceIdType.MESH
NT = (((1,), (1,)), ((), ()))
ORDER = [(0, 0), (0, 1), (1, 0), (7, 0), (1, 1), (7, 1), (2, 0), (6, 0), (2, 1), (6, 1), (3, 0), (5, 0), (3, 1), (5, 1), (4, 0), (4, 1)]
LEVELS = [(1, 6), (6, 10), (10, 16)]


def bin_index(x):
    guess = jnp.clip(jnp.ceil(x * (B / 9.0) + (B // 2 - 1)), 0.0, B - 1.0)
    edge_here = (guess + (1.0 - B // 2)) * (9.0 / B)
    edge_before = (guess - (1.0 * (B // 2))) * (9.0 / B)
    up = jnp.where((edge_here < x) & (guess < B - 1.0), 1.0, 0.0)
    down = jnp.where((edge_before >= x) & (guess > 0.0), 1.0, 0.0)
    return guess + up - down


def row_pack(tile, row):
    return jnp.broadcast_to(tile[row : row + 1, :], (16, 128)).astype(bf16)


def mask_tile(tile, bins):
    one, zero = jnp.ones((), bf16), jnp.zeros((), bf16)
    rows = []
    for i in range(OWN):
        halves = []
        for h in range(2):
            packed = row_pack(tile, h * 4 + i)
            halves.append(jnp.where(packed[None] <= bins, one, zero).reshape(B, 128))
        rows.append(jnp.concatenate(halves, axis=1))
    return jnp.concatenate(rows, axis=0)


def target_tile(tile, classes):
    zero = jnp.zeros((), bf16)
    parts = [[], []]
    for h in range(2):
        hit = row_pack(tile, h * 4)[None] == classes
        for n in range(NODES):
            weight = jnp.broadcast_to(row_pack(tile, h * 4 + 1 + n)[None], hit.shape)
            parts[n].append(jnp.where(hit, weight, zero).reshape(C, 128))
    return jnp.concatenate([jnp.concatenate(p, axis=1) for p in parts], axis=0)


def ratio(values):
    return jnp.sum(values * values, axis=0, keepdims=True) / jnp.maximum(jnp.sum(values, axis=0, keepdims=True), 1.0)


def kernel(
    feat_hbm, lab_hbm, wei_hbm, node_hbm, out_ref,
    feat_v, lab_v, wei_v, node_v, send, zbuf, rbuf, acc, m1s, m1, m2s, m2,
    relay, in_sem, s1_send, s1_recv, s2_send, s2_recv, m1_send, m1_recv, m2_send, m2_recv,
):
    my_rows, my_feat = lax.axis_index("rows"), lax.axis_index("feat")
    z, y = lax.div(my_rows, Y), lax.rem(my_rows, Y)

    def rows_peer(dz, dy):
        return lax.rem(z + dz, Z) * Y + lax.rem(y + dy, Y)

    def feat_peer(d):
        return lax.rem(my_feat + d, FEAT_AX)

    barrier = pltpu.get_barrier_semaphore()
    for dz, dy in ORDER[slice(*LEVELS[0])]:
        pl.semaphore_signal(barrier, inc=1, device_id={"rows": rows_peer(dz, dy)}, device_id_type=MESH)
    for d in range(1, FEAT_AX):
        pl.semaphore_signal(barrier, inc=1, device_id={"feat": feat_peer(d)}, device_id_type=MESH)

    loads = [
        pltpu.make_async_copy(lab_hbm, lab_v, in_sem.at[CHUNKS]),
        pltpu.make_async_copy(wei_hbm, wei_v, in_sem.at[CHUNKS + 1]),
        pltpu.make_async_copy(node_hbm, node_v, in_sem.at[CHUNKS + 2]),
    ]
    chunk_loads = []
    for q in range(CHUNKS):
        part = pl.ds(q * (512 // CHUNKS), 512 // CHUNKS)
        chunk_loads.append(pltpu.make_async_copy(feat_hbm.at[part], feat_v.at[part], in_sem.at[q]))
    for load in loads + chunk_loads:
        load.start()
    for load in loads:
        load.wait()

    label = lab_v[...].astype(f32)
    weight = wei_v[...].astype(f32)
    node = node_v[...]
    w0 = jnp.where(node == 0, weight, 0.0)
    w1 = jnp.where(node == 1, weight, 0.0)
    pad = jnp.zeros_like(w0)
    lines = []
    for h in range(2):
        cut = slice(h * 128, (h + 1) * 128)
        lines += [label[:, cut], w0[:, cut], w1[:, cut], pad[:, cut]]
    codes = jnp.concatenate(lines, axis=0).astype(bf16)
    sub = lax.broadcasted_iota(jnp.int32, (4, 8, 128), 1)

    def binned(r):
        values = bin_index(feat_v[pl.ds(pl.multiple_of(r * 32, 32), 32), :])
        a = values[:, :128].reshape(4, 8, 128)
        b = values[:, 128:].reshape(4, 8, 128)
        first = jnp.where(sub < 4, a, pltpu.roll(b, 4, 1))
        second = jnp.where(sub < 4, pltpu.roll(a, 4, 1), b)
        return jnp.stack([first, second], axis=1).reshape(8, 8, 128).astype(bf16)

    def place(r, carry):
        send[r, :FEAT_AX] = binned(r)
        send[r, FEAT_AX] = codes
        return carry

    for q in range(CHUNKS):
        chunk_loads[q].wait()
        lax.fori_loop(q * (ROWS_AX // CHUNKS), (q + 1) * (ROWS_AX // CHUNKS), place, 0)
    zbuf[0, :FEAT_AX] = binned(my_rows)
    zbuf[0, FEAT_AX] = codes
    acc[...] = jnp.zeros_like(acc)

    def forward(s, wait=True):
        if wait:
            pltpu.make_async_copy(zbuf.at[s], zbuf.at[s], s1_recv.at[s]).wait()
        for d in range(1, FEAT_AX):
            peer = feat_peer(d)
            for part, block in ((0, peer), (1, FEAT_AX)):
                pltpu.make_async_remote_copy(
                    src_ref=zbuf.at[s, block], dst_ref=rbuf.at[s, d, part], send_sem=s2_send, recv_sem=s2_recv.at[s],
                    device_id={"feat": peer}, device_id_type=MESH).start()

    bins = (lax.broadcasted_iota(jnp.int32, (8, 16, 128), 0) * 16 + lax.broadcasted_iota(jnp.int32, (8, 16, 128), 1)).astype(f32).astype(bf16)
    classes = bins[: C // 16]

    def use(start, count):
        masks, targets = [], []
        for u in range(count):
            part = rbuf.at[start + u, pl.ds(1, FEAT_AX - 1)]
            pltpu.make_async_copy(part, part, s2_recv.at[start + u]).wait()
        for u in range(count):
            s = start + u
            masks.append(mask_tile(zbuf[s, my_feat].astype(f32), bins))
            targets.append(target_tile(zbuf[s, FEAT_AX].astype(f32), classes))
            for d in range(1, FEAT_AX):
                masks.append(mask_tile(rbuf[s, d, 0].astype(f32), bins))
                targets.append(target_tile(rbuf[s, d, 1].astype(f32), classes))
        acc[...] += lax.dot_general(jnp.concatenate(masks, axis=1), jnp.concatenate(targets, axis=1), NT, preferred_element_type=f32)

    def send_level(k):
        for s in range(*LEVELS[k]):
            peer = rows_peer(*ORDER[s])
            pltpu.make_async_remote_copy(
                src_ref=send.at[peer], dst_ref=zbuf.at[s], send_sem=s1_send, recv_sem=s1_recv.at[s],
                device_id={"rows": peer}, device_id_type=MESH).start()

    def tell(k, side):
        peer = rows_peer(((k + 1) if side == 0 else (Z - 1 - k)), 0)
        pl.semaphore_signal(relay.at[k, side], inc=1, device_id={"rows": peer}, device_id_type=MESH)

    def forward_all(first, last):
        for s in range(first, last):
            forward(s, wait=s > 0)

    pl.semaphore_wait(barrier, LEVELS[0][1] - LEVELS[0][0] + FEAT_AX - 1)
    for side in range(2):
        tell(0, side)
    send_level(0)
    forward_all(0, 1)
    for side in range(2):
        pl.semaphore_wait(relay.at[0, side], 1)
    for side in range(2):
        tell(1, side)
    send_level(1)
    forward_all(1, 4)
    use(0, 1)
    for side in range(2):
        pl.semaphore_wait(relay.at[1, side], 1)
    send_level(2)
    forward_all(4, 6)

    def step(g, carry):
        @pl.when(g < 5)
        def _():
            forward(6 + 2 * g)
            forward(7 + 2 * g)

        use(1 + 2 * g, 2)
        return carry

    lax.fori_loop(0, 7, step, 0)
    use(15, 1)

    row_at = lax.broadcasted_iota(jnp.int32, (8, 128), 0)
    lane_at = lax.broadcasted_iota(jnp.int32, (8, 128), 1)
    gains = jnp.zeros((8, 128), f32)
    best = jnp.zeros((1, 128), f32)
    lane_row = lax.broadcasted_iota(jnp.int32, (1, 128), 1)
    for n in range(NODES):
        node_top = None
        for i in range(OWN):
            left = acc[i * B : (i + 1) * B, :].T[n * C : (n + 1) * C, :]
            total = left[:, B - 1 : B]
            right = total - left
            gain = ratio(left) + ratio(right) - ratio(total)
            top = jnp.max(gain, axis=1, keepdims=True)
            gains = jnp.where((row_at == n) & (lane_at == i), top, gains)
            node_top = top if node_top is None else jnp.maximum(node_top, top)
        best = jnp.where(lane_row == n, node_top, best)

    m1s[...] = best
    for d in range(1, FEAT_AX):
        pltpu.make_async_remote_copy(
            src_ref=m1s, dst_ref=m1.at[d], send_sem=m1_send, recv_sem=m1_recv,
            device_id={"feat": feat_peer(d)}, device_id_type=MESH).start()
    m1_all, m2_all = m1.at[pl.ds(1, FEAT_AX - 1)], m2.at[pl.ds(1, ROWS_AX - 1)]
    pltpu.make_async_copy(m1_all, m1_all, m1_recv).wait()
    best = jnp.maximum(best, jnp.max(m1[1:], axis=0))
    m2s[...] = best
    for s in range(1, ROWS_AX):
        pltpu.make_async_remote_copy(
            src_ref=m2s, dst_ref=m2.at[s], send_sem=m2_send, recv_sem=m2_recv,
            device_id={"rows": rows_peer(*ORDER[s])}, device_id_type=MESH).start()
    z_all, r_all = zbuf.at[pl.ds(1, ROWS_AX - 1)], rbuf.at[:, pl.ds(1, FEAT_AX - 1)]
    pltpu.make_async_copy(z_all, z_all, s1_send).wait()
    pltpu.make_async_copy(r_all, r_all, s2_send).wait()
    pltpu.make_async_copy(m1_all, m1_all, m1_send).wait()
    pltpu.make_async_copy(m2_all, m2_all, m2_send).wait()
    pltpu.make_async_copy(m2_all, m2_all, m2_recv).wait()
    best = jnp.maximum(best, jnp.max(m2[1:], axis=0))
    best_column = jnp.where(row_at == 0, best[:, 0:1], best[:, 1:2])
    out_ref[...] = jnp.where(lane_at < OWN, gains, best_column)


def local(features, labels, weights, nodes):
    dma = pltpu.SemaphoreType.DMA
    result = pl.pallas_call(
        kernel,
        out_shape=jax.ShapeDtypeStruct((8, 128), f32),
        in_specs=[pl.BlockSpec(memory_space=pl.ANY)] * 4,
        out_specs=pl.BlockSpec(memory_space=pltpu.VMEM),
        scratch_shapes=[
            pltpu.VMEM((512, LOCAL), f32),
            pltpu.VMEM((1, LOCAL), jnp.int32),
            pltpu.VMEM((1, LOCAL), bf16),
            pltpu.VMEM((1, LOCAL), jnp.int32),
            pltpu.VMEM((ROWS_AX, FEAT_AX + 1, 8, 128), bf16),
            pltpu.VMEM((ROWS_AX, FEAT_AX + 1, 8, 128), bf16),
            pltpu.VMEM((ROWS_AX, FEAT_AX, 2, 8, 128), bf16),
            pltpu.VMEM((OWN * B, NODES * C), f32),
            pltpu.VMEM((1, 128), f32),
            pltpu.VMEM((FEAT_AX, 1, 128), f32),
            pltpu.VMEM((1, 128), f32),
            pltpu.VMEM((ROWS_AX, 1, 128), f32),
            pltpu.SemaphoreType.REGULAR((len(LEVELS) - 1, 2)),
            dma((CHUNKS + 3,)), dma(()), dma((ROWS_AX,)), dma(()), dma((ROWS_AX,)), dma(()), dma(()), dma(()), dma(()),
        ],
        compiler_params=pltpu.CompilerParams(collective_id=0, has_side_effects=True, vmem_limit_bytes=48 * 1024 * 1024),
        name="split_scores",
    )(*[pltpu.with_memory_space_constraint(v, pltpu.HBM) for v in (features, labels.reshape(1, -1), weights, nodes)])
    return result[None, :NODES, :OWN], result[:NODES, OWN][None]


def solution(mesh):
    return jax.shard_map(
        local,
        mesh=mesh,
        in_specs=(
            P(None, ("rows", "feat")),
            P(("rows", "feat")),
            P("leaf", ("rows", "feat")),
            P("leaf", ("rows", "feat")),
        ),
        out_specs=(P("leaf", None, ("rows", "feat")), P("leaf", None)),
        check_vma=False,
    )
```

```python
import jax
import jax.numpy as jnp
from jax import lax
from jax.experimental import pallas as pl
from jax.experimental.pallas import tpu as pltpu
from jax.sharding import PartitionSpec as P

B = 128
C = 64
NODES = 2
OWN = 4
Z = 8
Y = 2
X = 4
CORES = 2
ROWS_AX = Z * Y
CHUNKS = 4
FEAT_AX = X * CORES
LOCAL = 256
f32 = jnp.float32
bf16 = jnp.bfloat16
MESH = pl.DeviceIdType.MESH
NT = (((1,), (1,)), ((), ()))
ORDER = [(0, 0), (0, 1), (1, 0), (7, 0), (1, 1), (7, 1), (2, 0), (6, 0), (2, 1), (6, 1), (3, 0), (5, 0), (3, 1), (5, 1), (4, 0), (4, 1)]
LEVELS = [(4, 6), (6, 10), (10, 16)]
DIRECT = (1, 4)


def bin_index(x):
    guess = jnp.clip(jnp.ceil(x * (B / 9.0) + (B // 2 - 1)), 0.0, B - 1.0)
    edge_here = (guess + (1.0 - B // 2)) * (9.0 / B)
    edge_before = (guess - (1.0 * (B // 2))) * (9.0 / B)
    up = jnp.where((edge_here < x) & (guess < B - 1.0), 1.0, 0.0)
    down = jnp.where((edge_before >= x) & (guess > 0.0), 1.0, 0.0)
    return guess + up - down


def row_pack(tile, row):
    return jnp.broadcast_to(tile[row : row + 1, :], (16, 128)).astype(bf16)


def mask_tile(tile, bins):
    one, zero = jnp.ones((), bf16), jnp.zeros((), bf16)
    rows = []
    for i in range(OWN):
        halves = []
        for h in range(2):
            packed = row_pack(tile, h * 4 + i)
            halves.append(jnp.where(packed[None] <= bins, one, zero).reshape(B, 128))
        rows.append(jnp.concatenate(halves, axis=1))
    return jnp.concatenate(rows, axis=0)


def target_tile(tile, classes):
    zero = jnp.zeros((), bf16)
    parts = [[], []]
    for h in range(2):
        hit = row_pack(tile, h * 4)[None] == classes
        for n in range(NODES):
            weight = jnp.broadcast_to(row_pack(tile, h * 4 + 1 + n)[None], hit.shape)
            parts[n].append(jnp.where(hit, weight, zero).reshape(C, 128))
    return jnp.concatenate([jnp.concatenate(p, axis=1) for p in parts], axis=0)


def ratio(values):
    return jnp.sum(values * values, axis=0, keepdims=True) / jnp.maximum(jnp.sum(values, axis=0, keepdims=True), 1.0)


def kernel(
    feat_hbm, lab_hbm, wei_hbm, node_hbm, out_ref,
    feat_v, lab_v, wei_v, node_v, send, zbuf, rbuf, acc, m1s, m1, m2s, m2,
    relay, in_sem, s0_send, s1_send, s1_recv, s2_send, s2_recv, m1_send, m1_recv, m2_send, m2_recv,
):
    my_rows, my_feat = lax.axis_index("rows"), lax.axis_index("feat")
    z, y = lax.div(my_rows, Y), lax.rem(my_rows, Y)

    def rows_peer(dz, dy):
        return lax.rem(z + dz, Z) * Y + lax.rem(y + dy, Y)

    def feat_peer(d):
        return lax.rem(my_feat + d, FEAT_AX)

    barrier = pltpu.get_barrier_semaphore()
    for dz, dy in ORDER[LEVELS[0][0] : LEVELS[0][1]]:
        pl.semaphore_signal(barrier, inc=1, device_id={"rows": rows_peer(dz, dy)}, device_id_type=MESH)
    for dz, dy in ORDER[: DIRECT[1]]:
        for d in range(FEAT_AX):
            if (dz, dy, d) != (0, 0, 0):
                pl.semaphore_signal(barrier, inc=1, device_id={"rows": rows_peer(dz, dy), "feat": feat_peer(d)}, device_id_type=MESH)

    loads = [
        pltpu.make_async_copy(lab_hbm, lab_v, in_sem.at[CHUNKS]),
        pltpu.make_async_copy(wei_hbm, wei_v, in_sem.at[CHUNKS + 1]),
        pltpu.make_async_copy(node_hbm, node_v, in_sem.at[CHUNKS + 2]),
    ]
    chunk_loads = []
    for q in range(CHUNKS):
        part = pl.ds(q * (512 // CHUNKS), 512 // CHUNKS)
        chunk_loads.append(pltpu.make_async_copy(feat_hbm.at[part], feat_v.at[part], in_sem.at[q]))
    for load in loads + chunk_loads:
        load.start()
    for load in loads:
        load.wait()

    label = lab_v[...].astype(f32)
    weight = wei_v[...].astype(f32)
    node = node_v[...]
    w0 = jnp.where(node == 0, weight, 0.0)
    w1 = jnp.where(node == 1, weight, 0.0)
    pad = jnp.zeros_like(w0)
    lines = []
    for h in range(2):
        cut = slice(h * 128, (h + 1) * 128)
        lines += [label[:, cut], w0[:, cut], w1[:, cut], pad[:, cut]]
    codes = jnp.concatenate(lines, axis=0).astype(bf16)
    sub = lax.broadcasted_iota(jnp.int32, (4, 8, 128), 1)

    def binned(r):
        values = bin_index(feat_v[pl.ds(pl.multiple_of(r * 32, 32), 32), :])
        a = values[:, :128].reshape(4, 8, 128)
        b = values[:, 128:].reshape(4, 8, 128)
        first = jnp.where(sub < 4, a, pltpu.roll(b, 4, 1))
        second = jnp.where(sub < 4, pltpu.roll(a, 4, 1), b)
        return jnp.stack([first, second], axis=1).reshape(8, 8, 128).astype(bf16)

    def place(r, carry):
        send[r, :FEAT_AX] = binned(r)
        send[r, FEAT_AX] = codes
        return carry

    for q in range(CHUNKS):
        chunk_loads[q].wait()
        lax.fori_loop(q * (ROWS_AX // CHUNKS), (q + 1) * (ROWS_AX // CHUNKS), place, 0)
    zbuf[0, :FEAT_AX] = binned(my_rows)
    zbuf[0, FEAT_AX] = codes
    acc[...] = jnp.zeros_like(acc)

    def forward(s, wait=True):
        if wait:
            pltpu.make_async_copy(zbuf.at[s], zbuf.at[s], s1_recv.at[s]).wait()
        for d in range(1, FEAT_AX):
            peer = feat_peer(d)
            for part, block in ((0, peer), (1, FEAT_AX)):
                pltpu.make_async_remote_copy(
                    src_ref=zbuf.at[s, block], dst_ref=rbuf.at[s, d, part], send_sem=s2_send, recv_sem=s2_recv.at[s],
                    device_id={"feat": peer}, device_id_type=MESH).start()

    bins = (lax.broadcasted_iota(jnp.int32, (8, 16, 128), 0) * 16 + lax.broadcasted_iota(jnp.int32, (8, 16, 128), 1)).astype(f32).astype(bf16)
    classes = bins[: C // 16]

    def use(start, count):
        masks, targets = [], []
        for u in range(count):
            part = rbuf.at[start + u, pl.ds(1, FEAT_AX - 1)]
            pltpu.make_async_copy(part, part, s2_recv.at[start + u]).wait()
        for u in range(count):
            s = start + u
            masks.append(mask_tile(zbuf[s, my_feat].astype(f32), bins))
            targets.append(target_tile(zbuf[s, FEAT_AX].astype(f32), classes))
            for d in range(1, FEAT_AX):
                masks.append(mask_tile(rbuf[s, d, 0].astype(f32), bins))
                targets.append(target_tile(rbuf[s, d, 1].astype(f32), classes))
        acc[...] += lax.dot_general(jnp.concatenate(masks, axis=1), jnp.concatenate(targets, axis=1), NT, preferred_element_type=f32)

    def send_level(k):
        for s in range(*LEVELS[k]):
            peer = rows_peer(*ORDER[s])
            pltpu.make_async_remote_copy(
                src_ref=send.at[peer], dst_ref=zbuf.at[s], send_sem=s1_send, recv_sem=s1_recv.at[s],
                device_id={"rows": peer}, device_id_type=MESH).start()

    def tell(k, side):
        peer = rows_peer(((k + 1) if side == 0 else (Z - 1 - k)), 0)
        pl.semaphore_signal(relay.at[k, side], inc=1, device_id={"rows": peer}, device_id_type=MESH)

    pl.semaphore_wait(barrier, LEVELS[0][1] - LEVELS[0][0] + DIRECT[1] * FEAT_AX - 1)
    for side in range(2):
        tell(0, side)
    for s in range(*DIRECT):
        rows = rows_peer(*ORDER[s])
        for d in range(FEAT_AX):
            feat = feat_peer(d)
            for part, block in ((0, feat), (1, FEAT_AX)):
                pltpu.make_async_remote_copy(
                    src_ref=send.at[rows, block],
                    dst_ref=zbuf.at[s, block] if d == 0 else rbuf.at[s, d, part],
                    send_sem=s0_send if d == 0 else s2_send,
                    recv_sem=s1_recv.at[s] if d == 0 else s2_recv.at[s],
                    device_id={"rows": rows, "feat": feat}, device_id_type=MESH).start()
    forward(0, wait=False)
    send_level(0)
    for side in range(2):
        pl.semaphore_wait(relay.at[0, side], 1)
    for side in range(2):
        tell(1, side)
    send_level(1)
    for side in range(2):
        pl.semaphore_wait(relay.at[1, side], 1)
    send_level(2)
    forward(4)
    forward(5)
    use(0, 1)
    for s in range(*DIRECT):
        part = zbuf.at[s, pl.ds(0, 2)]
        pltpu.make_async_copy(part, part, s1_recv.at[s]).wait()

    def step(g, carry):
        @pl.when(g < 5)
        def _():
            forward(6 + 2 * g)
            forward(7 + 2 * g)

        use(1 + 2 * g, 2)
        return carry

    lax.fori_loop(0, 7, step, 0)
    use(15, 1)

    row_at = lax.broadcasted_iota(jnp.int32, (8, 128), 0)
    lane_at = lax.broadcasted_iota(jnp.int32, (8, 128), 1)
    gains = jnp.zeros((8, 128), f32)
    best = jnp.zeros((1, 128), f32)
    lane_row = lax.broadcasted_iota(jnp.int32, (1, 128), 1)
    for n in range(NODES):
        node_top = None
        for i in range(OWN):
            left = acc[i * B : (i + 1) * B, :].T[n * C : (n + 1) * C, :]
            total = left[:, B - 1 : B]
            right = total - left
            gain = ratio(left) + ratio(right) - ratio(total)
            top = jnp.max(gain, axis=1, keepdims=True)
            gains = jnp.where((row_at == n) & (lane_at == i), top, gains)
            node_top = top if node_top is None else jnp.maximum(node_top, top)
        best = jnp.where(lane_row == n, node_top, best)

    m1s[...] = best
    for d in range(1, FEAT_AX):
        pltpu.make_async_remote_copy(
            src_ref=m1s, dst_ref=m1.at[d], send_sem=m1_send, recv_sem=m1_recv,
            device_id={"feat": feat_peer(d)}, device_id_type=MESH).start()
    m1_all, m2_all = m1.at[pl.ds(1, FEAT_AX - 1)], m2.at[pl.ds(1, ROWS_AX - 1)]
    pltpu.make_async_copy(m1_all, m1_all, m1_recv).wait()
    best = jnp.maximum(best, jnp.max(m1[1:], axis=0))
    m2s[...] = best
    for s in range(1, ROWS_AX):
        pltpu.make_async_remote_copy(
            src_ref=m2s, dst_ref=m2.at[s], send_sem=m2_send, recv_sem=m2_recv,
            device_id={"rows": rows_peer(*ORDER[s])}, device_id_type=MESH).start()
    z_near, z_all = zbuf.at[pl.ds(DIRECT[0], DIRECT[1] - DIRECT[0]), pl.ds(0, 2)], zbuf.at[pl.ds(DIRECT[1], ROWS_AX - DIRECT[1])]
    r_all = rbuf.at[:, pl.ds(1, FEAT_AX - 1)]
    pltpu.make_async_copy(z_near, z_near, s0_send).wait()
    pltpu.make_async_copy(z_all, z_all, s1_send).wait()
    pltpu.make_async_copy(r_all, r_all, s2_send).wait()
    pltpu.make_async_copy(m1_all, m1_all, m1_send).wait()
    pltpu.make_async_copy(m2_all, m2_all, m2_send).wait()
    pltpu.make_async_copy(m2_all, m2_all, m2_recv).wait()
    best = jnp.maximum(best, jnp.max(m2[1:], axis=0))
    best_column = jnp.where(row_at == 0, best[:, 0:1], best[:, 1:2])
    out_ref[...] = jnp.where(lane_at < OWN, gains, best_column)


def local(features, labels, weights, nodes):
    dma = pltpu.SemaphoreType.DMA
    result = pl.pallas_call(
        kernel,
        out_shape=jax.ShapeDtypeStruct((8, 128), f32),
        in_specs=[pl.BlockSpec(memory_space=pl.ANY)] * 4,
        out_specs=pl.BlockSpec(memory_space=pltpu.VMEM),
        scratch_shapes=[
            pltpu.VMEM((512, LOCAL), f32),
            pltpu.VMEM((1, LOCAL), jnp.int32),
            pltpu.VMEM((1, LOCAL), bf16),
            pltpu.VMEM((1, LOCAL), jnp.int32),
            pltpu.VMEM((ROWS_AX, FEAT_AX + 1, 8, 128), bf16),
            pltpu.VMEM((ROWS_AX, FEAT_AX + 1, 8, 128), bf16),
            pltpu.VMEM((ROWS_AX, FEAT_AX, 2, 8, 128), bf16),
            pltpu.VMEM((OWN * B, NODES * C), f32),
            pltpu.VMEM((1, 128), f32),
            pltpu.VMEM((FEAT_AX, 1, 128), f32),
            pltpu.VMEM((1, 128), f32),
            pltpu.VMEM((ROWS_AX, 1, 128), f32),
            pltpu.SemaphoreType.REGULAR((len(LEVELS) - 1, 2)),
            dma((CHUNKS + 3,)), dma(()), dma(()), dma((ROWS_AX,)), dma(()), dma((ROWS_AX,)), dma(()), dma(()), dma(()), dma(()),
        ],
        compiler_params=pltpu.CompilerParams(collective_id=0, has_side_effects=True, vmem_limit_bytes=48 * 1024 * 1024),
        name="split_scores",
    )(*[pltpu.with_memory_space_constraint(v, pltpu.HBM) for v in (features, labels.reshape(1, -1), weights, nodes)])
    return result[None, :NODES, :OWN], jnp.max(result[None, :NODES, OWN : 2 * OWN], axis=2)


def solution(mesh):
    return jax.shard_map(
        local,
        mesh=mesh,
        in_specs=(
            P(None, ("rows", "feat")),
            P(("rows", "feat")),
            P("leaf", ("rows", "feat")),
            P("leaf", ("rows", "feat")),
        ),
        out_specs=(P("leaf", None, ("rows", "feat")), P("leaf", None)),
        check_vma=False,
    )
```

```python
import jax
import jax.numpy as jnp
from jax import lax
from jax.experimental import pallas as pl
from jax.experimental.pallas import tpu as pltpu
from jax.sharding import PartitionSpec as P

B = 128
C = 64
NODES = 2
OWN = 4
Z = 8
Y = 2
X = 4
CORES = 2
ROWS_AX = Z * Y
CHUNKS = 4
FEAT_AX = X * CORES
LOCAL = 256
f32 = jnp.float32
bf16 = jnp.bfloat16
MESH = pl.DeviceIdType.MESH
NT = (((1,), (1,)), ((), ()))
ORDER = [(0, 0), (0, 1), (1, 0), (7, 0), (1, 1), (7, 1), (2, 0), (6, 0), (2, 1), (6, 1), (3, 0), (5, 0), (3, 1), (5, 1), (4, 0), (4, 1)]
LEVELS = [(1, 6), (6, 10), (10, 16)]


def bin_index(x):
    guess = jnp.clip(jnp.ceil(x * (B / 9.0) + (B // 2 - 1)), 0.0, B - 1.0)
    edge_here = (guess + (1.0 - B // 2)) * (9.0 / B)
    edge_before = (guess - (1.0 * (B // 2))) * (9.0 / B)
    up = jnp.where((edge_here < x) & (guess < B - 1.0), 1.0, 0.0)
    down = jnp.where((edge_before >= x) & (guess > 0.0), 1.0, 0.0)
    return guess + up - down


def row_pack(tile, row):
    return jnp.broadcast_to(tile[row : row + 1, :], (16, 128)).astype(bf16)


def mask_tile(tile, bins):
    one, zero = jnp.ones((), bf16), jnp.zeros((), bf16)
    rows = []
    for i in range(OWN):
        halves = []
        for h in range(2):
            packed = row_pack(tile, h * 4 + i)
            halves.append(jnp.where(packed[None] <= bins, one, zero).reshape(B, 128))
        rows.append(jnp.concatenate(halves, axis=1))
    return jnp.concatenate(rows, axis=0)


def target_tile(tile, classes):
    zero = jnp.zeros((), bf16)
    parts = [[], []]
    for h in range(2):
        hit = row_pack(tile, h * 4)[None] == classes
        for n in range(NODES):
            weight = jnp.broadcast_to(row_pack(tile, h * 4 + 1 + n)[None], hit.shape)
            parts[n].append(jnp.where(hit, weight, zero).reshape(C, 128))
    return jnp.concatenate([jnp.concatenate(p, axis=1) for p in parts], axis=0)


def ratio(values):
    return jnp.sum(values * values, axis=0, keepdims=True) / jnp.maximum(jnp.sum(values, axis=0, keepdims=True), 1.0)


def kernel(
    feat_hbm, lab_hbm, wei_hbm, node_hbm, out_ref,
    feat_v, lab_v, wei_v, node_v, send, zbuf, rbuf, acc, m1s, m1, m2s, m2,
    relay, in_sem, s1_send, s1_recv, s2_send, s2_recv, m1_send, m1_recv, m2_send, m2_recv,
):
    my_rows, my_feat = lax.axis_index("rows"), lax.axis_index("feat")
    z, y = lax.div(my_rows, Y), lax.rem(my_rows, Y)

    def rows_peer(dz, dy):
        return lax.rem(z + dz, Z) * Y + lax.rem(y + dy, Y)

    def feat_peer(d):
        return lax.rem(my_feat + d, FEAT_AX)

    barrier = pltpu.get_barrier_semaphore()
    for dz, dy in ORDER[slice(*LEVELS[0])]:
        pl.semaphore_signal(barrier, inc=1, device_id={"rows": rows_peer(dz, dy)}, device_id_type=MESH)
    for d in range(1, FEAT_AX):
        pl.semaphore_signal(barrier, inc=1, device_id={"feat": feat_peer(d)}, device_id_type=MESH)

    loads = [
        pltpu.make_async_copy(lab_hbm, lab_v, in_sem.at[CHUNKS]),
        pltpu.make_async_copy(wei_hbm, wei_v, in_sem.at[CHUNKS + 1]),
        pltpu.make_async_copy(node_hbm, node_v, in_sem.at[CHUNKS + 2]),
    ]
    chunk_loads = []
    for q in range(CHUNKS):
        part = pl.ds(q * (512 // CHUNKS), 512 // CHUNKS)
        chunk_loads.append(pltpu.make_async_copy(feat_hbm.at[part], feat_v.at[part], in_sem.at[q]))
    for load in loads + chunk_loads:
        load.start()
    for load in loads:
        load.wait()

    label = lab_v[...].astype(f32)
    weight = wei_v[...].astype(f32)
    node = node_v[...]
    w0 = jnp.where(node == 0, weight, 0.0)
    w1 = jnp.where(node == 1, weight, 0.0)
    pad = jnp.zeros_like(w0)
    lines = []
    for h in range(2):
        cut = slice(h * 128, (h + 1) * 128)
        lines += [label[:, cut], w0[:, cut], w1[:, cut], pad[:, cut]]
    codes = jnp.concatenate(lines, axis=0).astype(bf16)
    sub = lax.broadcasted_iota(jnp.int32, (4, 8, 128), 1)

    def binned(r):
        values = bin_index(feat_v[pl.ds(pl.multiple_of(r * 32, 32), 32), :])
        a = values[:, :128].reshape(4, 8, 128)
        b = values[:, 128:].reshape(4, 8, 128)
        first = jnp.where(sub < 4, a, pltpu.roll(b, 4, 1))
        second = jnp.where(sub < 4, pltpu.roll(a, 4, 1), b)
        return jnp.stack([first, second], axis=1).reshape(8, 8, 128).astype(bf16)

    def place(r, carry):
        send[r, :FEAT_AX] = binned(r)
        send[r, FEAT_AX] = codes
        return carry

    for q in range(CHUNKS):
        chunk_loads[q].wait()
        lax.fori_loop(q * (ROWS_AX // CHUNKS), (q + 1) * (ROWS_AX // CHUNKS), place, 0)
    zbuf[0, :FEAT_AX] = binned(my_rows)
    zbuf[0, FEAT_AX] = codes
    acc[...] = jnp.zeros_like(acc)

    def forward(s, wait=True):
        if wait:
            pltpu.make_async_copy(zbuf.at[s], zbuf.at[s], s1_recv.at[s]).wait()
        for d in range(1, FEAT_AX):
            peer = feat_peer(d)
            for part, block in ((0, peer), (1, FEAT_AX)):
                pltpu.make_async_remote_copy(
                    src_ref=zbuf.at[s, block], dst_ref=rbuf.at[s, d, part], send_sem=s2_send, recv_sem=s2_recv.at[s],
                    device_id={"feat": peer}, device_id_type=MESH).start()

    bins = (lax.broadcasted_iota(jnp.int32, (8, 16, 128), 0) * 16 + lax.broadcasted_iota(jnp.int32, (8, 16, 128), 1)).astype(f32).astype(bf16)
    classes = bins[: C // 16]

    def use(start, count):
        masks, targets = [], []
        for u in range(count):
            part = rbuf.at[start + u, pl.ds(1, FEAT_AX - 1)]
            pltpu.make_async_copy(part, part, s2_recv.at[start + u]).wait()
        for u in range(count):
            s = start + u
            masks.append(mask_tile(zbuf[s, my_feat].astype(f32), bins))
            targets.append(target_tile(zbuf[s, FEAT_AX].astype(f32), classes))
            for d in range(1, FEAT_AX):
                masks.append(mask_tile(rbuf[s, d, 0].astype(f32), bins))
                targets.append(target_tile(rbuf[s, d, 1].astype(f32), classes))
        acc[...] += lax.dot_general(jnp.concatenate(masks, axis=1), jnp.concatenate(targets, axis=1), NT, preferred_element_type=f32)

    def send_level(k):
        for s in range(*LEVELS[k]):
            peer = rows_peer(*ORDER[s])
            pltpu.make_async_remote_copy(
                src_ref=send.at[peer], dst_ref=zbuf.at[s], send_sem=s1_send, recv_sem=s1_recv.at[s],
                device_id={"rows": peer}, device_id_type=MESH).start()

    def tell(k, side):
        peer = rows_peer(((k + 1) if side == 0 else (Z - 1 - k)), 0)
        pl.semaphore_signal(relay.at[k, side], inc=1, device_id={"rows": peer}, device_id_type=MESH)

    def forward_all(first, last):
        for s in range(first, last):
            forward(s, wait=s > 0)

    pl.semaphore_wait(barrier, LEVELS[0][1] - LEVELS[0][0] + FEAT_AX - 1)
    for side in range(2):
        tell(0, side)
    send_level(0)
    forward_all(0, 1)
    for side in range(2):
        pl.semaphore_wait(relay.at[0, side], 1)
    for side in range(2):
        tell(1, side)
    send_level(1)
    for side in range(2):
        pl.semaphore_wait(relay.at[1, side], 1)
    send_level(2)
    forward_all(1, 4)
    use(0, 1)
    forward_all(4, 6)

    def step(g, carry):
        @pl.when(g < 5)
        def _():
            forward(6 + 2 * g)
            forward(7 + 2 * g)

        use(1 + 2 * g, 2)
        return carry

    lax.fori_loop(0, 7, step, 0)
    use(15, 1)

    row_at = lax.broadcasted_iota(jnp.int32, (8, 128), 0)
    lane_at = lax.broadcasted_iota(jnp.int32, (8, 128), 1)
    gains = jnp.zeros((8, 128), f32)
    best = jnp.zeros((1, 128), f32)
    lane_row = lax.broadcasted_iota(jnp.int32, (1, 128), 1)
    for n in range(NODES):
        node_top = None
        for i in range(OWN):
            left = acc[i * B : (i + 1) * B, :].T[n * C : (n + 1) * C, :]
            total = left[:, B - 1 : B]
            right = total - left
            gain = ratio(left) + ratio(right) - ratio(total)
            top = jnp.max(gain, axis=1, keepdims=True)
            gains = jnp.where((row_at == n) & (lane_at == i), top, gains)
            node_top = top if node_top is None else jnp.maximum(node_top, top)
        best = jnp.where(lane_row == n, node_top, best)

    m1s[...] = best
    for d in range(1, FEAT_AX):
        pltpu.make_async_remote_copy(
            src_ref=m1s, dst_ref=m1.at[d], send_sem=m1_send, recv_sem=m1_recv,
            device_id={"feat": feat_peer(d)}, device_id_type=MESH).start()
    m1_all, m2_all = m1.at[pl.ds(1, FEAT_AX - 1)], m2.at[pl.ds(1, ROWS_AX - 1)]
    pltpu.make_async_copy(m1_all, m1_all, m1_recv).wait()
    best = jnp.maximum(best, jnp.max(m1[1:], axis=0))
    m2s[...] = best
    for s in range(1, ROWS_AX):
        pltpu.make_async_remote_copy(
            src_ref=m2s, dst_ref=m2.at[s], send_sem=m2_send, recv_sem=m2_recv,
            device_id={"rows": rows_peer(*ORDER[s])}, device_id_type=MESH).start()
    z_all, r_all = zbuf.at[pl.ds(1, ROWS_AX - 1)], rbuf.at[:, pl.ds(1, FEAT_AX - 1)]
    pltpu.make_async_copy(z_all, z_all, s1_send).wait()
    pltpu.make_async_copy(r_all, r_all, s2_send).wait()
    pltpu.make_async_copy(m1_all, m1_all, m1_send).wait()
    pltpu.make_async_copy(m2_all, m2_all, m2_send).wait()
    pltpu.make_async_copy(m2_all, m2_all, m2_recv).wait()
    best = jnp.maximum(best, jnp.max(m2[1:], axis=0))
    best_column = jnp.where(row_at == 0, best[:, 0:1], best[:, 1:2])
    out_ref[...] = jnp.where(lane_at < OWN, gains, best_column)


def local(features, labels, weights, nodes):
    dma = pltpu.SemaphoreType.DMA
    result = pl.pallas_call(
        kernel,
        out_shape=jax.ShapeDtypeStruct((8, 128), f32),
        in_specs=[pl.BlockSpec(memory_space=pl.ANY)] * 4,
        out_specs=pl.BlockSpec(memory_space=pltpu.VMEM),
        scratch_shapes=[
            pltpu.VMEM((512, LOCAL), f32),
            pltpu.VMEM((1, LOCAL), jnp.int32),
            pltpu.VMEM((1, LOCAL), bf16),
            pltpu.VMEM((1, LOCAL), jnp.int32),
            pltpu.VMEM((ROWS_AX, FEAT_AX + 1, 8, 128), bf16),
            pltpu.VMEM((ROWS_AX, FEAT_AX + 1, 8, 128), bf16),
            pltpu.VMEM((ROWS_AX, FEAT_AX, 2, 8, 128), bf16),
            pltpu.VMEM((OWN * B, NODES * C), f32),
            pltpu.VMEM((1, 128), f32),
            pltpu.VMEM((FEAT_AX, 1, 128), f32),
            pltpu.VMEM((1, 128), f32),
            pltpu.VMEM((ROWS_AX, 1, 128), f32),
            pltpu.SemaphoreType.REGULAR((len(LEVELS) - 1, 2)),
            dma((CHUNKS + 3,)), dma(()), dma((ROWS_AX,)), dma(()), dma((ROWS_AX,)), dma(()), dma(()), dma(()), dma(()),
        ],
        compiler_params=pltpu.CompilerParams(collective_id=0, has_side_effects=True, vmem_limit_bytes=48 * 1024 * 1024),
        name="split_scores",
    )(*[pltpu.with_memory_space_constraint(v, pltpu.HBM) for v in (features, labels.reshape(1, -1), weights, nodes)])
    return result[None, :NODES, :OWN], jnp.max(result[None, :NODES, OWN : 2 * OWN], axis=2)


def solution(mesh):
    return jax.shard_map(
        local,
        mesh=mesh,
        in_specs=(
            P(None, ("rows", "feat")),
            P(("rows", "feat")),
            P("leaf", ("rows", "feat")),
            P("leaf", ("rows", "feat")),
        ),
        out_specs=(P("leaf", None, ("rows", "feat")), P("leaf", None)),
        check_vma=False,
    )
```

```python
import jax
import jax.numpy as jnp
from jax import lax
from jax.experimental import pallas as pl
from jax.experimental.pallas import tpu as pltpu
from jax.sharding import PartitionSpec as P

B = 128
C = 64
NODES = 2
OWN = 4
Z = 8
Y = 2
X = 4
CORES = 2
ROWS_AX = Z * Y
CHUNKS = 4
FEAT_AX = X * CORES
LOCAL = 256
f32 = jnp.float32
bf16 = jnp.bfloat16
MESH = pl.DeviceIdType.MESH
NT = (((1,), (1,)), ((), ()))
ORDER = [(0, 0), (0, 1), (1, 0), (7, 0), (1, 1), (7, 1), (2, 0), (6, 0), (2, 1), (6, 1), (3, 0), (5, 0), (3, 1), (5, 1), (4, 0), (4, 1)]
NEAR = 6


def bin_index(x):
    guess = jnp.clip(jnp.ceil(x * (B / 9.0) + (B // 2 - 1)), 0.0, B - 1.0)
    edge_here = (guess + (1.0 - B // 2)) * (9.0 / B)
    edge_before = (guess - (1.0 * (B // 2))) * (9.0 / B)
    up = jnp.where((edge_here < x) & (guess < B - 1.0), 1.0, 0.0)
    down = jnp.where((edge_before >= x) & (guess > 0.0), 1.0, 0.0)
    return guess + up - down


def row_pack(tile, row):
    return jnp.broadcast_to(tile[row : row + 1, :], (16, 128)).astype(bf16)


def mask_tile(tile, bins):
    one, zero = jnp.ones((), bf16), jnp.zeros((), bf16)
    rows = []
    for i in range(OWN):
        halves = []
        for h in range(2):
            packed = row_pack(tile, h * 4 + i)
            halves.append(jnp.where(packed[None] <= bins, one, zero).reshape(B, 128))
        rows.append(jnp.concatenate(halves, axis=1))
    return jnp.concatenate(rows, axis=0)


def target_tile(tile, classes):
    zero = jnp.zeros((), bf16)
    parts = [[], []]
    for h in range(2):
        hit = row_pack(tile, h * 4)[None] == classes
        for n in range(NODES):
            weight = jnp.broadcast_to(row_pack(tile, h * 4 + 1 + n)[None], hit.shape)
            parts[n].append(jnp.where(hit, weight, zero).reshape(C, 128))
    return jnp.concatenate([jnp.concatenate(p, axis=1) for p in parts], axis=0)


def ratio(values):
    return jnp.sum(values * values, axis=0, keepdims=True) / jnp.maximum(jnp.sum(values, axis=0, keepdims=True), 1.0)


def kernel(
    feat_hbm, lab_hbm, wei_hbm, node_hbm, out_ref,
    feat_v, lab_v, wei_v, node_v, send, own_codes, rbuf, acc, top_row, tops,
    in_sem, feat_recv, code_recv, far_recv, top_recv, sent,
):
    my_rows, my_feat = lax.axis_index("rows"), lax.axis_index("feat")
    z, y = lax.div(my_rows, Y), lax.rem(my_rows, Y)

    def rows_peer(s):
        dz, dy = ORDER[s]
        return lax.rem(z + dz, Z) * Y + lax.rem(y + dy, Y)

    def feat_peer(d):
        return lax.rem(my_feat + d, FEAT_AX)

    def to_column(s, action):
        rows = rows_peer(s)

        def one(d, carry):
            action(rows, feat_peer(d), d)
            return carry

        lax.fori_loop(1 if s == 0 else 0, FEAT_AX, one, 0)

    def push(source, target, send_sem, recv_sem, rows, feat):
        pltpu.make_async_remote_copy(
            src_ref=source, dst_ref=target, send_sem=send_sem, recv_sem=recv_sem,
            device_id={"rows": rows, "feat": feat}, device_id_type=MESH).start()

    def wait_all(part, sem):
        pltpu.make_async_copy(part, part, sem).wait()

    loads = [
        pltpu.make_async_copy(lab_hbm, lab_v, in_sem.at[CHUNKS]),
        pltpu.make_async_copy(wei_hbm, wei_v, in_sem.at[CHUNKS + 1]),
        pltpu.make_async_copy(node_hbm, node_v, in_sem.at[CHUNKS + 2]),
    ]
    chunk_loads = []
    for q in range(CHUNKS):
        part = pl.ds(q * (512 // CHUNKS), 512 // CHUNKS)
        chunk_loads.append(pltpu.make_async_copy(feat_hbm.at[part], feat_v.at[part], in_sem.at[q]))
    for load in loads + chunk_loads:
        load.start()

    barrier = pltpu.get_barrier_semaphore()

    def greet(rows, feat, d):
        pl.semaphore_signal(barrier, inc=1, device_id={"rows": rows, "feat": feat}, device_id_type=MESH)

    for s in reversed(range(ROWS_AX)):
        to_column(s, greet)
    for load in loads:
        load.wait()

    label = lab_v[...].astype(f32)
    weight = wei_v[...].astype(f32)
    node = node_v[...]
    w0 = jnp.where(node == 0, weight, 0.0)
    w1 = jnp.where(node == 1, weight, 0.0)
    pad = jnp.zeros_like(w0)
    lines = []
    for h in range(2):
        cut = slice(h * 128, (h + 1) * 128)
        lines += [label[:, cut], w0[:, cut], w1[:, cut], pad[:, cut]]
    codes = jnp.concatenate(lines, axis=0).astype(bf16)
    sub = lax.broadcasted_iota(jnp.int32, (4, 8, 128), 1)

    def binned(r):
        values = bin_index(feat_v[pl.ds(pl.multiple_of(r * 32, 32), 32), :])
        a = values[:, :128].reshape(4, 8, 128)
        b = values[:, 128:].reshape(4, 8, 128)
        first = jnp.where(sub < 4, a, pltpu.roll(b, 4, 1))
        second = jnp.where(sub < 4, pltpu.roll(a, 4, 1), b)
        return jnp.stack([first, second], axis=1).reshape(8, 8, 128).astype(bf16)

    def place(r, carry):
        send[r] = binned(r)
        return carry

    own_codes[...] = codes
    rbuf[0, 0, 1] = codes
    for q in range(CHUNKS):
        chunk_loads[q].wait()
        lax.fori_loop(q * (ROWS_AX // CHUNKS), (q + 1) * (ROWS_AX // CHUNKS), place, 0)
    rbuf[0, 0, 0] = send[my_rows, my_feat]
    acc[...] = jnp.zeros_like(acc)

    bins = (lax.broadcasted_iota(jnp.int32, (8, 16, 128), 0) * 16 + lax.broadcasted_iota(jnp.int32, (8, 16, 128), 1)).astype(f32).astype(bf16)
    classes = bins[: C // 16]

    def use(start, count):
        masks, targets = [], []
        for u in range(count):
            s = start + u
            for d in range(FEAT_AX):
                masks.append(mask_tile(rbuf[s, d, 0].astype(f32), bins))
                targets.append(target_tile(rbuf[s, d, 1].astype(f32), classes))
        acc[...] += lax.dot_general(jnp.concatenate(masks, axis=1), jnp.concatenate(targets, axis=1), NT, preferred_element_type=f32)

    others = pl.ds(1, FEAT_AX - 1)

    def push_features(s):
        def one(rows, feat, d):
            push(send.at[rows, feat], rbuf.at[s, d, 0], sent.at[0 if s == 0 else 1], feat_recv.at[s], rows, feat)

        to_column(s, one)

    def push_codes(s):
        def one(rows, feat, d):
            push(own_codes, rbuf.at[s, d, 1], sent.at[2 if s == 0 else 3], code_recv.at[s], rows, feat)

        to_column(s, one)

    pl.semaphore_wait(barrier, ROWS_AX * FEAT_AX - 1)
    for s in range(NEAR):
        push_codes(s)
        push_features(s)
        if s == 1:
            for far in range(NEAR, ROWS_AX):
                push(own_codes, rbuf.at[far, 0, 1], sent.at[4], far_recv.at[far], rows_peer(far), my_feat)
    for s in range(NEAR, ROWS_AX):
        push_features(s)

    wait_all(rbuf.at[0, others, 0], feat_recv.at[0])
    wait_all(rbuf.at[0, others, 1], code_recv.at[0])
    wait_all(rbuf.at[1, :, 0], feat_recv.at[1])
    wait_all(rbuf.at[1, :, 1], code_recv.at[1])
    use(0, 2)

    def pass_on(s, carry):
        wait_all(rbuf.at[s, 0, 1], far_recv.at[s])

        def one(d, inner):
            push(rbuf.at[s, 0, 1], rbuf.at[s, d, 1], sent.at[5], code_recv.at[s], my_rows, feat_peer(d))
            return inner

        lax.fori_loop(1, FEAT_AX, one, 0)
        return carry

    lax.fori_loop(NEAR, ROWS_AX, pass_on, 0)

    def step(g, carry):
        for u in range(2):
            s = 2 * g + u
            wait_all(rbuf.at[s, :, 0], feat_recv.at[s])

            @pl.when(g < NEAR // 2)
            def _():
                wait_all(rbuf.at[s, :, 1], code_recv.at[s])

            @pl.when(g >= NEAR // 2)
            def _():
                wait_all(rbuf.at[s, others, 1], code_recv.at[s])

        use(2 * g, 2)
        return carry

    lax.fori_loop(1, ROWS_AX // 2, step, 0)

    row_at = lax.broadcasted_iota(jnp.int32, (8, 128), 0)
    lane_at = lax.broadcasted_iota(jnp.int32, (8, 128), 1)
    gains = jnp.zeros((8, 128), f32)
    best = jnp.zeros((1, 128), f32)
    lane_row = lax.broadcasted_iota(jnp.int32, (1, 128), 1)
    for n in range(NODES):
        node_top = None
        for i in range(OWN):
            left = acc[i * B : (i + 1) * B, :].T[n * C : (n + 1) * C, :]
            total = left[:, B - 1 : B]
            right = total - left
            gain = ratio(left) + ratio(right) - ratio(total)
            top = jnp.max(gain, axis=1, keepdims=True)
            gains = jnp.where((row_at == n) & (lane_at == i), top, gains)
            node_top = top if node_top is None else jnp.maximum(node_top, top)
        best = jnp.where(lane_row == n, node_top, best)

    top_row[...] = best

    def push_top(s):
        def one(rows, feat, d):
            push(top_row, tops.at[s, d], sent.at[6 if s == 0 else 7], top_recv.at[0 if s == 0 else 1], rows, feat)

        to_column(s, one)

    for s in reversed(range(ROWS_AX)):
        push_top(s)
    rest, far_rest = pl.ds(1, ROWS_AX - 1), pl.ds(NEAR, ROWS_AX - NEAR)
    wait_all(rbuf.at[0, others, 0], sent.at[0])
    wait_all(rbuf.at[rest, :, 0], sent.at[1])
    wait_all(rbuf.at[0, others, 1], sent.at[2])
    wait_all(rbuf.at[pl.ds(1, NEAR - 1), :, 1], sent.at[3])
    wait_all(rbuf.at[far_rest, 0, 1], sent.at[4])
    wait_all(rbuf.at[far_rest, others, 1], sent.at[5])
    wait_all(tops.at[0, others], sent.at[6])
    wait_all(tops.at[rest], sent.at[7])
    wait_all(tops.at[0, others], top_recv.at[0])
    wait_all(tops.at[rest], top_recv.at[1])
    best = jnp.maximum(best, jnp.maximum(jnp.max(tops[0, 1:], axis=0), jnp.max(tops[1:], axis=(0, 1))))
    best_column = jnp.where(row_at == 0, best[:, 0:1], best[:, 1:2])
    out_ref[...] = jnp.where(lane_at < OWN, gains, best_column)


def local(features, labels, weights, nodes):
    dma = pltpu.SemaphoreType.DMA
    result = pl.pallas_call(
        kernel,
        out_shape=jax.ShapeDtypeStruct((8, 128), f32),
        in_specs=[pl.BlockSpec(memory_space=pl.ANY)] * 4,
        out_specs=pl.BlockSpec(memory_space=pltpu.VMEM),
        scratch_shapes=[
            pltpu.VMEM((512, LOCAL), f32),
            pltpu.VMEM((1, LOCAL), jnp.int32),
            pltpu.VMEM((1, LOCAL), bf16),
            pltpu.VMEM((1, LOCAL), jnp.int32),
            pltpu.VMEM((ROWS_AX, FEAT_AX, 8, 128), bf16),
            pltpu.VMEM((8, 128), bf16),
            pltpu.VMEM((ROWS_AX, FEAT_AX, 2, 8, 128), bf16),
            pltpu.VMEM((OWN * B, NODES * C), f32),
            pltpu.VMEM((1, 128), f32),
            pltpu.VMEM((ROWS_AX, FEAT_AX, 1, 128), f32),
            dma((CHUNKS + 3,)), dma((ROWS_AX,)), dma((ROWS_AX,)), dma((ROWS_AX,)), dma((2,)), dma((8,)),
        ],
        compiler_params=pltpu.CompilerParams(collective_id=0, has_side_effects=True, vmem_limit_bytes=48 * 1024 * 1024),
        name="split_scores",
    )(*[pltpu.with_memory_space_constraint(v, pltpu.HBM) for v in (features, labels.reshape(1, -1), weights, nodes)])
    return result[None, :NODES, :OWN], jnp.max(result[None, :NODES, OWN : 2 * OWN], axis=2)


def solution(mesh):
    return jax.shard_map(
        local,
        mesh=mesh,
        in_specs=(
            P(None, ("rows", "feat")),
            P(("rows", "feat")),
            P("leaf", ("rows", "feat")),
            P("leaf", ("rows", "feat")),
        ),
        out_specs=(P("leaf", None, ("rows", "feat")), P("leaf", None)),
        check_vma=False,
    )
```

```python
import jax
import jax.numpy as jnp
from jax import lax
from jax.experimental import pallas as pl
from jax.experimental.pallas import tpu as pltpu
from jax.sharding import PartitionSpec as P

B = 128
C = 64
NODES = 2
OWN = 4
Z = 8
Y = 2
X = 4
CORES = 2
ROWS_AX = Z * Y
CHUNKS = 4
FEAT_AX = X * CORES
LOCAL = 256
f32 = jnp.float32
bf16 = jnp.bfloat16
MESH = pl.DeviceIdType.MESH
NT = (((1,), (1,)), ((), ()))
ORDER = [(0, 0), (0, 1), (1, 0), (7, 0), (1, 1), (7, 1), (2, 0), (6, 0), (2, 1), (6, 1), (3, 0), (5, 0), (3, 1), (5, 1), (4, 0), (4, 1)]
NEAR = 6


def bin_index(x):
    guess = jnp.clip(jnp.ceil(x * (B / 9.0) + (B // 2 - 1)), 0.0, B - 1.0)
    edge_here = (guess + (1.0 - B // 2)) * (9.0 / B)
    edge_before = (guess - (1.0 * (B // 2))) * (9.0 / B)
    up = jnp.where((edge_here < x) & (guess < B - 1.0), 1.0, 0.0)
    down = jnp.where((edge_before >= x) & (guess > 0.0), 1.0, 0.0)
    return guess + up - down


def row_pack(tile, row):
    return jnp.broadcast_to(tile[row : row + 1, :], (16, 128)).astype(bf16)


def mask_tile(tile, bins):
    one, zero = jnp.ones((), bf16), jnp.zeros((), bf16)
    rows = []
    for i in range(OWN):
        halves = []
        for h in range(2):
            packed = row_pack(tile, h * 4 + i)
            halves.append(jnp.where(packed[None] <= bins, one, zero).reshape(B, 128))
        rows.append(jnp.concatenate(halves, axis=1))
    return jnp.concatenate(rows, axis=0)


def target_tile(tile, classes):
    zero = jnp.zeros((), bf16)
    parts = [[], []]
    for h in range(2):
        hit = row_pack(tile, h * 4)[None] == classes
        for n in range(NODES):
            weight = jnp.broadcast_to(row_pack(tile, h * 4 + 1 + n)[None], hit.shape)
            parts[n].append(jnp.where(hit, weight, zero).reshape(C, 128))
    return jnp.concatenate([jnp.concatenate(p, axis=1) for p in parts], axis=0)


def ratio(values):
    return jnp.sum(values * values, axis=0, keepdims=True) / jnp.maximum(jnp.sum(values, axis=0, keepdims=True), 1.0)


def kernel(
    feat_hbm, lab_hbm, wei_hbm, node_hbm, out_ref,
    feat_v, lab_v, wei_v, node_v, send, own_codes, rbuf, acc, top_row, tops,
    in_sem, feat_recv, code_recv, far_recv, top_recv, sent,
):
    my_rows, my_feat = lax.axis_index("rows"), lax.axis_index("feat")
    z, y = lax.div(my_rows, Y), lax.rem(my_rows, Y)

    def rows_peer(s):
        dz, dy = ORDER[s]
        return lax.rem(z + dz, Z) * Y + lax.rem(y + dy, Y)

    def feat_peer(d):
        return lax.rem(my_feat + d, FEAT_AX)

    def to_column(s, action):
        rows = rows_peer(s)

        for d in range(1 if s == 0 else 0, FEAT_AX):
            action(rows, feat_peer(d), d)

    def push(source, target, send_sem, recv_sem, rows, feat):
        pltpu.make_async_remote_copy(
            src_ref=source, dst_ref=target, send_sem=send_sem, recv_sem=recv_sem,
            device_id={"rows": rows, "feat": feat}, device_id_type=MESH).start()

    def wait_all(part, sem):
        pltpu.make_async_copy(part, part, sem).wait()

    loads = [
        pltpu.make_async_copy(lab_hbm, lab_v, in_sem.at[CHUNKS]),
        pltpu.make_async_copy(wei_hbm, wei_v, in_sem.at[CHUNKS + 1]),
        pltpu.make_async_copy(node_hbm, node_v, in_sem.at[CHUNKS + 2]),
    ]
    chunk_loads = []
    for q in range(CHUNKS):
        part = pl.ds(q * (512 // CHUNKS), 512 // CHUNKS)
        chunk_loads.append(pltpu.make_async_copy(feat_hbm.at[part], feat_v.at[part], in_sem.at[q]))
    for load in loads + chunk_loads:
        load.start()

    barrier = pltpu.get_barrier_semaphore()

    def greet(rows, feat, d):
        pl.semaphore_signal(barrier, inc=1, device_id={"rows": rows, "feat": feat}, device_id_type=MESH)

    for s in reversed(range(ROWS_AX)):
        to_column(s, greet)
    for load in loads:
        load.wait()

    label = lab_v[...].astype(f32)
    weight = wei_v[...].astype(f32)
    node = node_v[...]
    w0 = jnp.where(node == 0, weight, 0.0)
    w1 = jnp.where(node == 1, weight, 0.0)
    pad = jnp.zeros_like(w0)
    lines = []
    for h in range(2):
        cut = slice(h * 128, (h + 1) * 128)
        lines += [label[:, cut], w0[:, cut], w1[:, cut], pad[:, cut]]
    codes = jnp.concatenate(lines, axis=0).astype(bf16)
    sub = lax.broadcasted_iota(jnp.int32, (4, 8, 128), 1)

    def binned(r):
        values = bin_index(feat_v[pl.ds(pl.multiple_of(r * 32, 32), 32), :])
        a = values[:, :128].reshape(4, 8, 128)
        b = values[:, 128:].reshape(4, 8, 128)
        first = jnp.where(sub < 4, a, pltpu.roll(b, 4, 1))
        second = jnp.where(sub < 4, pltpu.roll(a, 4, 1), b)
        return jnp.stack([first, second], axis=1).reshape(8, 8, 128).astype(bf16)

    def place(r, carry):
        send[r] = binned(r)
        return carry

    own_codes[...] = codes
    rbuf[0, 0, 1] = codes
    for q in range(CHUNKS):
        chunk_loads[q].wait()
        lax.fori_loop(q * (ROWS_AX // CHUNKS), (q + 1) * (ROWS_AX // CHUNKS), place, 0)
    rbuf[0, 0, 0] = send[my_rows, my_feat]
    acc[...] = jnp.zeros_like(acc)

    bins = (lax.broadcasted_iota(jnp.int32, (8, 16, 128), 0) * 16 + lax.broadcasted_iota(jnp.int32, (8, 16, 128), 1)).astype(f32).astype(bf16)
    classes = bins[: C // 16]

    def use(start, count):
        masks, targets = [], []
        for u in range(count):
            s = start + u
            for d in range(FEAT_AX):
                masks.append(mask_tile(rbuf[s, d, 0].astype(f32), bins))
                targets.append(target_tile(rbuf[s, d, 1].astype(f32), classes))
        acc[...] += lax.dot_general(jnp.concatenate(masks, axis=1), jnp.concatenate(targets, axis=1), NT, preferred_element_type=f32)

    others = pl.ds(1, FEAT_AX - 1)

    def push_features(s):
        def one(rows, feat, d):
            push(send.at[rows, feat], rbuf.at[s, d, 0], sent.at[0 if s == 0 else 1], feat_recv.at[s], rows, feat)

        to_column(s, one)

    def push_codes(s):
        def one(rows, feat, d):
            push(own_codes, rbuf.at[s, d, 1], sent.at[2 if s == 0 else 3], code_recv.at[s], rows, feat)

        to_column(s, one)

    pl.semaphore_wait(barrier, ROWS_AX * FEAT_AX - 1)
    for s in range(NEAR):
        push_codes(s)
        push_features(s)
        if s == 1:
            for far in range(NEAR, ROWS_AX):
                push(own_codes, rbuf.at[far, 0, 1], sent.at[4], far_recv.at[far], rows_peer(far), my_feat)
    for s in range(NEAR, ROWS_AX):
        push_features(s)

    wait_all(rbuf.at[0, others, 0], feat_recv.at[0])
    wait_all(rbuf.at[0, others, 1], code_recv.at[0])
    wait_all(rbuf.at[1, :, 0], feat_recv.at[1])
    wait_all(rbuf.at[1, :, 1], code_recv.at[1])
    use(0, 2)

    def pass_on(s, carry):
        wait_all(rbuf.at[s, 0, 1], far_recv.at[s])

        for d in range(1, FEAT_AX):
            push(rbuf.at[s, 0, 1], rbuf.at[s, d, 1], sent.at[5], code_recv.at[s], my_rows, feat_peer(d))
        return carry

    lax.fori_loop(NEAR, ROWS_AX, pass_on, 0)

    def step(g, carry):
        for u in range(2):
            s = 2 * g + u
            wait_all(rbuf.at[s, :, 0], feat_recv.at[s])

            @pl.when(g < NEAR // 2)
            def _():
                wait_all(rbuf.at[s, :, 1], code_recv.at[s])

            @pl.when(g >= NEAR // 2)
            def _():
                wait_all(rbuf.at[s, others, 1], code_recv.at[s])

        use(2 * g, 2)
        return carry

    lax.fori_loop(1, ROWS_AX // 2, step, 0)

    row_at = lax.broadcasted_iota(jnp.int32, (8, 128), 0)
    lane_at = lax.broadcasted_iota(jnp.int32, (8, 128), 1)
    gains = jnp.zeros((8, 128), f32)
    best = jnp.zeros((1, 128), f32)
    lane_row = lax.broadcasted_iota(jnp.int32, (1, 128), 1)
    for n in range(NODES):
        node_top = None
        for i in range(OWN):
            left = acc[i * B : (i + 1) * B, :].T[n * C : (n + 1) * C, :]
            total = left[:, B - 1 : B]
            right = total - left
            gain = ratio(left) + ratio(right) - ratio(total)
            top = jnp.max(gain, axis=1, keepdims=True)
            gains = jnp.where((row_at == n) & (lane_at == i), top, gains)
            node_top = top if node_top is None else jnp.maximum(node_top, top)
        best = jnp.where(lane_row == n, node_top, best)

    top_row[...] = best

    def push_top(s):
        def one(rows, feat, d):
            push(top_row, tops.at[s, d], sent.at[6 if s == 0 else 7], top_recv.at[0 if s == 0 else 1], rows, feat)

        to_column(s, one)

    for s in reversed(range(ROWS_AX)):
        push_top(s)
    rest, far_rest = pl.ds(1, ROWS_AX - 1), pl.ds(NEAR, ROWS_AX - NEAR)
    wait_all(rbuf.at[0, others, 0], sent.at[0])
    wait_all(rbuf.at[rest, :, 0], sent.at[1])
    wait_all(rbuf.at[0, others, 1], sent.at[2])
    wait_all(rbuf.at[pl.ds(1, NEAR - 1), :, 1], sent.at[3])
    wait_all(rbuf.at[far_rest, 0, 1], sent.at[4])
    wait_all(rbuf.at[far_rest, others, 1], sent.at[5])
    wait_all(tops.at[0, others], sent.at[6])
    wait_all(tops.at[rest], sent.at[7])
    wait_all(tops.at[0, others], top_recv.at[0])
    wait_all(tops.at[rest], top_recv.at[1])
    best = jnp.maximum(best, jnp.maximum(jnp.max(tops[0, 1:], axis=0), jnp.max(tops[1:], axis=(0, 1))))
    best_column = jnp.where(row_at == 0, best[:, 0:1], best[:, 1:2])
    out_ref[...] = jnp.where(lane_at < OWN, gains, best_column)


def local(features, labels, weights, nodes):
    dma = pltpu.SemaphoreType.DMA
    result = pl.pallas_call(
        kernel,
        out_shape=jax.ShapeDtypeStruct((8, 128), f32),
        in_specs=[pl.BlockSpec(memory_space=pl.ANY)] * 4,
        out_specs=pl.BlockSpec(memory_space=pltpu.VMEM),
        scratch_shapes=[
            pltpu.VMEM((512, LOCAL), f32),
            pltpu.VMEM((1, LOCAL), jnp.int32),
            pltpu.VMEM((1, LOCAL), bf16),
            pltpu.VMEM((1, LOCAL), jnp.int32),
            pltpu.VMEM((ROWS_AX, FEAT_AX, 8, 128), bf16),
            pltpu.VMEM((8, 128), bf16),
            pltpu.VMEM((ROWS_AX, FEAT_AX, 2, 8, 128), bf16),
            pltpu.VMEM((OWN * B, NODES * C), f32),
            pltpu.VMEM((1, 128), f32),
            pltpu.VMEM((ROWS_AX, FEAT_AX, 1, 128), f32),
            dma((CHUNKS + 3,)), dma((ROWS_AX,)), dma((ROWS_AX,)), dma((ROWS_AX,)), dma((2,)), dma((8,)),
        ],
        compiler_params=pltpu.CompilerParams(collective_id=0, has_side_effects=True, vmem_limit_bytes=48 * 1024 * 1024),
        name="split_scores",
    )(*[pltpu.with_memory_space_constraint(v, pltpu.HBM) for v in (features, labels.reshape(1, -1), weights, nodes)])
    return result[None, :NODES, :OWN], jnp.max(result[None, :NODES, OWN : 2 * OWN], axis=2)


def solution(mesh):
    return jax.shard_map(
        local,
        mesh=mesh,
        in_specs=(
            P(None, ("rows", "feat")),
            P(("rows", "feat")),
            P("leaf", ("rows", "feat")),
            P("leaf", ("rows", "feat")),
        ),
        out_specs=(P("leaf", None, ("rows", "feat")), P("leaf", None)),
        check_vma=False,
    )
```

```python
import jax
import jax.numpy as jnp
from jax import lax
from jax.experimental import pallas as pl
from jax.experimental.pallas import tpu as pltpu
from jax.sharding import PartitionSpec as P

B = 128
C = 64
NODES = 2
OWN = 4
Z = 8
Y = 2
X = 4
CORES = 2
ROWS_AX = Z * Y
CHUNKS = 4
FEAT_AX = X * CORES
LOCAL = 256
f32 = jnp.float32
bf16 = jnp.bfloat16
MESH = pl.DeviceIdType.MESH
NT = (((1,), (1,)), ((), ()))
ORDER = [(0, 0), (0, 1), (1, 0), (7, 0), (1, 1), (7, 1), (2, 0), (6, 0), (2, 1), (6, 1), (3, 0), (5, 0), (3, 1), (5, 1), (4, 0), (4, 1)]


def bin_index(x):
    guess = jnp.clip(jnp.ceil(x * (B / 9.0) + (B // 2 - 1)), 0.0, B - 1.0)
    edge_here = (guess + (1.0 - B // 2)) * (9.0 / B)
    edge_before = (guess - (1.0 * (B // 2))) * (9.0 / B)
    up = jnp.where((edge_here < x) & (guess < B - 1.0), 1.0, 0.0)
    down = jnp.where((edge_before >= x) & (guess > 0.0), 1.0, 0.0)
    return guess + up - down


def row_pack(tile, row):
    return jnp.broadcast_to(tile[row : row + 1, :], (16, 128)).astype(bf16)


def mask_tile(tile, bins):
    one, zero = jnp.ones((), bf16), jnp.zeros((), bf16)
    rows = []
    for i in range(OWN):
        halves = []
        for h in range(2):
            packed = row_pack(tile, h * 4 + i)
            halves.append(jnp.where(packed[None] <= bins, one, zero).reshape(B, 128))
        rows.append(jnp.concatenate(halves, axis=1))
    return jnp.concatenate(rows, axis=0)


def target_tile(tile, classes):
    zero = jnp.zeros((), bf16)
    parts = [[], []]
    for h in range(2):
        hit = row_pack(tile, h * 4)[None] == classes
        for n in range(NODES):
            weight = jnp.broadcast_to(row_pack(tile, h * 4 + 1 + n)[None], hit.shape)
            parts[n].append(jnp.where(hit, weight, zero).reshape(C, 128))
    return jnp.concatenate([jnp.concatenate(p, axis=1) for p in parts], axis=0)


def ratio(values):
    return jnp.sum(values * values, axis=0, keepdims=True) / jnp.maximum(jnp.sum(values, axis=0, keepdims=True), 1.0)


def kernel(
    feat_hbm, lab_hbm, wei_hbm, node_hbm, out_ref,
    feat_v, lab_v, wei_v, node_v, send, rbuf, acc, top_row, tops,
    in_sem, block_recv, top_recv, sent,
):
    my_rows, my_feat = lax.axis_index("rows"), lax.axis_index("feat")
    z, y = lax.div(my_rows, Y), lax.rem(my_rows, Y)

    def rows_peer(s):
        dz, dy = ORDER[s]
        return lax.rem(z + dz, Z) * Y + lax.rem(y + dy, Y)

    def feat_peer(d):
        return lax.rem(my_feat + d, FEAT_AX)

    def to_column(s, action):
        rows = rows_peer(s)

        def one(d, carry):
            action(rows, feat_peer(d), d)
            return carry

        lax.fori_loop(1 if s == 0 else 0, FEAT_AX, one, 0)

    def push(source, target, send_sem, recv_sem, rows, feat):
        pltpu.make_async_remote_copy(
            src_ref=source, dst_ref=target, send_sem=send_sem, recv_sem=recv_sem,
            device_id={"rows": rows, "feat": feat}, device_id_type=MESH).start()

    def wait_all(part, sem):
        pltpu.make_async_copy(part, part, sem).wait()

    loads = [
        pltpu.make_async_copy(lab_hbm, lab_v, in_sem.at[CHUNKS]),
        pltpu.make_async_copy(wei_hbm, wei_v, in_sem.at[CHUNKS + 1]),
        pltpu.make_async_copy(node_hbm, node_v, in_sem.at[CHUNKS + 2]),
    ]
    chunk_loads = []
    for q in range(CHUNKS):
        part = pl.ds(q * (512 // CHUNKS), 512 // CHUNKS)
        chunk_loads.append(pltpu.make_async_copy(feat_hbm.at[part], feat_v.at[part], in_sem.at[q]))
    for load in loads + chunk_loads:
        load.start()

    barrier = pltpu.get_barrier_semaphore()

    def greet(rows, feat, d):
        pl.semaphore_signal(barrier, inc=1, device_id={"rows": rows, "feat": feat}, device_id_type=MESH)

    for s in reversed(range(ROWS_AX)):
        to_column(s, greet)
    for load in loads:
        load.wait()

    label = lab_v[...].astype(f32)
    weight = wei_v[...].astype(f32)
    node = node_v[...]
    w0 = jnp.where(node == 0, weight, 0.0)
    w1 = jnp.where(node == 1, weight, 0.0)
    pad = jnp.zeros_like(w0)
    lines = []
    for h in range(2):
        cut = slice(h * 128, (h + 1) * 128)
        lines += [label[:, cut], w0[:, cut], w1[:, cut], pad[:, cut]]
    codes = jnp.concatenate(lines, axis=0).astype(bf16)
    sub = lax.broadcasted_iota(jnp.int32, (4, 8, 128), 1)

    def binned(r):
        values = bin_index(feat_v[pl.ds(pl.multiple_of(r * 32, 32), 32), :])
        a = values[:, :128].reshape(4, 8, 128)
        b = values[:, 128:].reshape(4, 8, 128)
        first = jnp.where(sub < 4, a, pltpu.roll(b, 4, 1))
        second = jnp.where(sub < 4, pltpu.roll(a, 4, 1), b)
        return jnp.stack([first, second], axis=1).reshape(8, 8, 128).astype(bf16)

    def place(r, carry):
        send[r, :, 0] = binned(r)
        send[r, :, 1] = jnp.broadcast_to(codes[None], (FEAT_AX, 8, 128))
        return carry

    for q in range(CHUNKS):
        chunk_loads[q].wait()
        lax.fori_loop(q * (ROWS_AX // CHUNKS), (q + 1) * (ROWS_AX // CHUNKS), place, 0)
    rbuf[0, 0] = send[my_rows, my_feat]
    acc[...] = jnp.zeros_like(acc)

    bins = (lax.broadcasted_iota(jnp.int32, (8, 16, 128), 0) * 16 + lax.broadcasted_iota(jnp.int32, (8, 16, 128), 1)).astype(f32).astype(bf16)
    classes = bins[: C // 16]

    def use(start, count):
        masks, targets = [], []
        for u in range(count):
            s = start + u
            for d in range(FEAT_AX):
                masks.append(mask_tile(rbuf[s, d, 0].astype(f32), bins))
                targets.append(target_tile(rbuf[s, d, 1].astype(f32), classes))
        acc[...] += lax.dot_general(jnp.concatenate(masks, axis=1), jnp.concatenate(targets, axis=1), NT, preferred_element_type=f32)

    others = pl.ds(1, FEAT_AX - 1)

    def push_blocks(s):
        def one(rows, feat, d):
            push(send.at[rows, feat], rbuf.at[s, d], sent.at[0 if s == 0 else 1], block_recv.at[s], rows, feat)

        to_column(s, one)

    pl.semaphore_wait(barrier, ROWS_AX * FEAT_AX - 1)
    for s in range(ROWS_AX):
        push_blocks(s)

    wait_all(rbuf.at[0, others], block_recv.at[0])
    wait_all(rbuf.at[1], block_recv.at[1])
    use(0, 2)

    def step(g, carry):
        for u in range(2):
            wait_all(rbuf.at[2 * g + u], block_recv.at[2 * g + u])
        use(2 * g, 2)
        return carry

    lax.fori_loop(1, ROWS_AX // 2, step, 0)

    row_at = lax.broadcasted_iota(jnp.int32, (8, 128), 0)
    lane_at = lax.broadcasted_iota(jnp.int32, (8, 128), 1)
    gains = jnp.zeros((8, 128), f32)
    best = jnp.zeros((1, 128), f32)
    lane_row = lax.broadcasted_iota(jnp.int32, (1, 128), 1)
    for n in range(NODES):
        node_top = None
        for i in range(OWN):
            left = acc[i * B : (i + 1) * B, :].T[n * C : (n + 1) * C, :]
            total = left[:, B - 1 : B]
            right = total - left
            gain = ratio(left) + ratio(right) - ratio(total)
            top = jnp.max(gain, axis=1, keepdims=True)
            gains = jnp.where((row_at == n) & (lane_at == i), top, gains)
            node_top = top if node_top is None else jnp.maximum(node_top, top)
        best = jnp.where(lane_row == n, node_top, best)

    top_row[...] = best

    def push_top(s):
        def one(rows, feat, d):
            push(top_row, tops.at[s, d], sent.at[2 if s == 0 else 3], top_recv.at[0 if s == 0 else 1], rows, feat)

        to_column(s, one)

    for s in reversed(range(ROWS_AX)):
        push_top(s)
    rest = pl.ds(1, ROWS_AX - 1)
    wait_all(rbuf.at[0, others], sent.at[0])
    wait_all(rbuf.at[rest], sent.at[1])
    wait_all(tops.at[0, others], sent.at[2])
    wait_all(tops.at[rest], sent.at[3])
    wait_all(tops.at[0, others], top_recv.at[0])
    wait_all(tops.at[rest], top_recv.at[1])
    best = jnp.maximum(best, jnp.maximum(jnp.max(tops[0, 1:], axis=0), jnp.max(tops[1:], axis=(0, 1))))
    best_column = jnp.where(row_at == 0, best[:, 0:1], best[:, 1:2])
    out_ref[...] = jnp.where(lane_at < OWN, gains, best_column)


def local(features, labels, weights, nodes):
    dma = pltpu.SemaphoreType.DMA
    result = pl.pallas_call(
        kernel,
        out_shape=jax.ShapeDtypeStruct((8, 128), f32),
        in_specs=[pl.BlockSpec(memory_space=pl.ANY)] * 4,
        out_specs=pl.BlockSpec(memory_space=pltpu.VMEM),
        scratch_shapes=[
            pltpu.VMEM((512, LOCAL), f32),
            pltpu.VMEM((1, LOCAL), jnp.int32),
            pltpu.VMEM((1, LOCAL), bf16),
            pltpu.VMEM((1, LOCAL), jnp.int32),
            pltpu.VMEM((ROWS_AX, FEAT_AX, 2, 8, 128), bf16),
            pltpu.VMEM((ROWS_AX, FEAT_AX, 2, 8, 128), bf16),
            pltpu.VMEM((OWN * B, NODES * C), f32),
            pltpu.VMEM((1, 128), f32),
            pltpu.VMEM((ROWS_AX, FEAT_AX, 1, 128), f32),
            dma((CHUNKS + 3,)), dma((ROWS_AX,)), dma((2,)), dma((4,)),
        ],
        compiler_params=pltpu.CompilerParams(collective_id=0, has_side_effects=True, vmem_limit_bytes=48 * 1024 * 1024),
        name="split_scores",
    )(*[pltpu.with_memory_space_constraint(v, pltpu.HBM) for v in (features, labels.reshape(1, -1), weights, nodes)])
    return result[None, :NODES, :OWN], jnp.max(result[None, :NODES, OWN : 2 * OWN], axis=2)


def solution(mesh):
    return jax.shard_map(
        local,
        mesh=mesh,
        in_specs=(
            P(None, ("rows", "feat")),
            P(("rows", "feat")),
            P("leaf", ("rows", "feat")),
            P("leaf", ("rows", "feat")),
        ),
        out_specs=(P("leaf", None, ("rows", "feat")), P("leaf", None)),
        check_vma=False,
    )
```

```python
import jax
import jax.numpy as jnp
from jax import lax
from jax.experimental import pallas as pl
from jax.experimental.pallas import tpu as pltpu
from jax.sharding import PartitionSpec as P

B = 128
C = 64
NODES = 2
OWN = 4
Z = 8
Y = 2
X = 4
CORES = 2
ROWS_AX = Z * Y
CHUNKS = 4
FEAT_AX = X * CORES
LOCAL = 256
f32 = jnp.float32
bf16 = jnp.bfloat16
MESH = pl.DeviceIdType.MESH
NT = (((1,), (1,)), ((), ()))
ORDER = [(0, 0), (0, 1), (1, 0), (7, 0), (1, 1), (7, 1), (2, 0), (6, 0), (2, 1), (6, 1), (3, 0), (5, 0), (3, 1), (5, 1), (4, 0), (4, 1)]
LEVELS = [(1, 6), (6, 10), (10, 16)]


def bin_index(x):
    guess = jnp.clip(jnp.ceil(x * (B / 9.0) + (B // 2 - 1)), 0.0, B - 1.0)
    edge_here = (guess + (1.0 - B // 2)) * (9.0 / B)
    edge_before = (guess - (1.0 * (B // 2))) * (9.0 / B)
    up = jnp.where((edge_here < x) & (guess < B - 1.0), 1.0, 0.0)
    down = jnp.where((edge_before >= x) & (guess > 0.0), 1.0, 0.0)
    return guess + up - down


def row_pack(tile, row):
    return jnp.broadcast_to(tile[row : row + 1, :], (16, 128)).astype(bf16)


def mask_tile(tile, bins):
    one, zero = jnp.ones((), bf16), jnp.zeros((), bf16)
    rows = []
    for i in range(OWN):
        halves = []
        for h in range(2):
            packed = row_pack(tile, h * 4 + i)
            halves.append(jnp.where(packed[None] <= bins, one, zero).reshape(B, 128))
        rows.append(jnp.concatenate(halves, axis=1))
    return jnp.concatenate(rows, axis=0)


def target_tile(tile, classes):
    zero = jnp.zeros((), bf16)
    parts = [[], []]
    for h in range(2):
        hit = row_pack(tile, h * 4)[None] == classes
        for n in range(NODES):
            weight = jnp.broadcast_to(row_pack(tile, h * 4 + 1 + n)[None], hit.shape)
            parts[n].append(jnp.where(hit, weight, zero).reshape(C, 128))
    return jnp.concatenate([jnp.concatenate(p, axis=1) for p in parts], axis=0)


def ratio(values):
    return jnp.sum(values * values, axis=0, keepdims=True) / jnp.maximum(jnp.sum(values, axis=0, keepdims=True), 1.0)


def kernel(
    feat_hbm, lab_hbm, wei_hbm, node_hbm, out_ref,
    feat_v, lab_v, wei_v, node_v, send, zbuf, rbuf, acc, top_row, tops,
    relay, in_sem, s1_send, s1_recv, s2_send, s2_recv, near_send, near_recv, top_send, top_recv,
):
    my_rows, my_feat = lax.axis_index("rows"), lax.axis_index("feat")
    z, y = lax.div(my_rows, Y), lax.rem(my_rows, Y)

    def rows_peer(dz, dy):
        return lax.rem(z + dz, Z) * Y + lax.rem(y + dy, Y)

    def feat_peer(d):
        return lax.rem(my_feat + d, FEAT_AX)

    barrier = pltpu.get_barrier_semaphore()
    for dz, dy in ORDER[slice(*LEVELS[0])]:
        pl.semaphore_signal(barrier, inc=1, device_id={"rows": rows_peer(dz, dy)}, device_id_type=MESH)
    for d in range(1, FEAT_AX):
        pl.semaphore_signal(barrier, inc=1, device_id={"feat": feat_peer(d)}, device_id_type=MESH)

    loads = [
        pltpu.make_async_copy(lab_hbm, lab_v, in_sem.at[CHUNKS]),
        pltpu.make_async_copy(wei_hbm, wei_v, in_sem.at[CHUNKS + 1]),
        pltpu.make_async_copy(node_hbm, node_v, in_sem.at[CHUNKS + 2]),
    ]
    chunk_loads = []
    for q in range(CHUNKS):
        part = pl.ds(q * (512 // CHUNKS), 512 // CHUNKS)
        chunk_loads.append(pltpu.make_async_copy(feat_hbm.at[part], feat_v.at[part], in_sem.at[q]))
    for load in loads + chunk_loads:
        load.start()
    for load in loads:
        load.wait()

    label = lab_v[...].astype(f32)
    weight = wei_v[...].astype(f32)
    node = node_v[...]
    w0 = jnp.where(node == 0, weight, 0.0)
    w1 = jnp.where(node == 1, weight, 0.0)
    pad = jnp.zeros_like(w0)
    lines = []
    for h in range(2):
        cut = slice(h * 128, (h + 1) * 128)
        lines += [label[:, cut], w0[:, cut], w1[:, cut], pad[:, cut]]
    codes = jnp.concatenate(lines, axis=0).astype(bf16)
    sub = lax.broadcasted_iota(jnp.int32, (4, 8, 128), 1)

    def binned(r):
        values = bin_index(feat_v[pl.ds(pl.multiple_of(r * 32, 32), 32), :])
        a = values[:, :128].reshape(4, 8, 128)
        b = values[:, 128:].reshape(4, 8, 128)
        first = jnp.where(sub < 4, a, pltpu.roll(b, 4, 1))
        second = jnp.where(sub < 4, pltpu.roll(a, 4, 1), b)
        return jnp.stack([first, second], axis=1).reshape(8, 8, 128).astype(bf16)

    def place(r, carry):
        send[r, :FEAT_AX] = binned(r)
        send[r, FEAT_AX] = codes
        return carry

    for q in range(CHUNKS):
        chunk_loads[q].wait()
        lax.fori_loop(q * (ROWS_AX // CHUNKS), (q + 1) * (ROWS_AX // CHUNKS), place, 0)
    zbuf[0, :FEAT_AX] = binned(my_rows)
    zbuf[0, FEAT_AX] = codes
    acc[...] = jnp.zeros_like(acc)

    def forward(s, wait=True):
        if wait:
            pltpu.make_async_copy(zbuf.at[s], zbuf.at[s], s1_recv.at[s]).wait()
        for d in range(1, FEAT_AX):
            peer = feat_peer(d)
            for part, block in ((0, peer), (1, FEAT_AX)):
                pltpu.make_async_remote_copy(
                    src_ref=zbuf.at[s, block], dst_ref=rbuf.at[s, d, part], send_sem=s2_send, recv_sem=s2_recv.at[s],
                    device_id={"feat": peer}, device_id_type=MESH).start()

    bins = (lax.broadcasted_iota(jnp.int32, (8, 16, 128), 0) * 16 + lax.broadcasted_iota(jnp.int32, (8, 16, 128), 1)).astype(f32).astype(bf16)
    classes = bins[: C // 16]

    def use(start, count):
        masks, targets = [], []
        for u in range(count):
            part = rbuf.at[start + u, pl.ds(1, FEAT_AX - 1)]
            pltpu.make_async_copy(part, part, s2_recv.at[start + u]).wait()
        for u in range(count):
            s = start + u
            masks.append(mask_tile(zbuf[s, my_feat].astype(f32), bins))
            targets.append(target_tile(zbuf[s, FEAT_AX].astype(f32), classes))
            for d in range(1, FEAT_AX):
                masks.append(mask_tile(rbuf[s, d, 0].astype(f32), bins))
                targets.append(target_tile(rbuf[s, d, 1].astype(f32), classes))
        acc[...] += lax.dot_general(jnp.concatenate(masks, axis=1), jnp.concatenate(targets, axis=1), NT, preferred_element_type=f32)

    def send_level(k):
        for s in range(*LEVELS[k]):
            peer = rows_peer(*ORDER[s])
            pltpu.make_async_remote_copy(
                src_ref=send.at[peer], dst_ref=zbuf.at[s], send_sem=s1_send, recv_sem=s1_recv.at[s],
                device_id={"rows": peer}, device_id_type=MESH).start()

    def tell(k, side):
        peer = rows_peer(((k + 1) if side == 0 else (Z - 1 - k)), 0)
        pl.semaphore_signal(relay.at[k, side], inc=1, device_id={"rows": peer}, device_id_type=MESH)

    def forward_all(first, last):
        for s in range(first, last):
            forward(s, wait=s > 0)

    pl.semaphore_wait(barrier, LEVELS[0][1] - LEVELS[0][0] + FEAT_AX - 1)
    for side in range(2):
        tell(0, side)
    send_level(0)
    forward_all(0, 1)
    for side in range(2):
        pl.semaphore_wait(relay.at[0, side], 1)
    for side in range(2):
        tell(1, side)
    send_level(1)
    for side in range(2):
        pl.semaphore_wait(relay.at[1, side], 1)
    send_level(2)
    forward_all(1, 4)
    use(0, 1)
    forward_all(4, 6)

    def step(g, carry):
        @pl.when(g < 5)
        def _():
            forward(6 + 2 * g)
            forward(7 + 2 * g)

        use(1 + 2 * g, 2)
        return carry

    lax.fori_loop(0, 7, step, 0)
    use(15, 1)

    row_at = lax.broadcasted_iota(jnp.int32, (8, 128), 0)
    lane_at = lax.broadcasted_iota(jnp.int32, (8, 128), 1)
    gains = jnp.zeros((8, 128), f32)
    best = jnp.zeros((1, 128), f32)
    lane_row = lax.broadcasted_iota(jnp.int32, (1, 128), 1)
    for n in range(NODES):
        node_top = None
        for i in range(OWN):
            left = acc[i * B : (i + 1) * B, :].T[n * C : (n + 1) * C, :]
            total = left[:, B - 1 : B]
            right = total - left
            gain = ratio(left) + ratio(right) - ratio(total)
            top = jnp.max(gain, axis=1, keepdims=True)
            gains = jnp.where((row_at == n) & (lane_at == i), top, gains)
            node_top = top if node_top is None else jnp.maximum(node_top, top)
        best = jnp.where(lane_row == n, node_top, best)

    top_row[...] = best
    for s in reversed(range(ROWS_AX)):
        rows = rows_peer(*ORDER[s])

        def push_top(d, carry, s=s, rows=rows):
            pltpu.make_async_remote_copy(
                src_ref=top_row, dst_ref=tops.at[s, d],
                send_sem=near_send if s == 0 else top_send, recv_sem=near_recv if s == 0 else top_recv,
                device_id={"rows": rows, "feat": feat_peer(d)}, device_id_type=MESH).start()
            return carry

        lax.fori_loop(1 if s == 0 else 0, FEAT_AX, push_top, 0)
    z_all, r_all = zbuf.at[pl.ds(1, ROWS_AX - 1)], rbuf.at[:, pl.ds(1, FEAT_AX - 1)]
    pltpu.make_async_copy(z_all, z_all, s1_send).wait()
    pltpu.make_async_copy(r_all, r_all, s2_send).wait()
    near_tops, far_tops = tops.at[0, pl.ds(1, FEAT_AX - 1)], tops.at[pl.ds(1, ROWS_AX - 1)]
    pltpu.make_async_copy(near_tops, near_tops, near_send).wait()
    pltpu.make_async_copy(far_tops, far_tops, top_send).wait()
    pltpu.make_async_copy(near_tops, near_tops, near_recv).wait()
    pltpu.make_async_copy(far_tops, far_tops, top_recv).wait()
    best = jnp.maximum(best, jnp.maximum(jnp.max(tops[0, 1:], axis=0), jnp.max(tops[1:], axis=(0, 1))))
    best_column = jnp.where(row_at == 0, best[:, 0:1], best[:, 1:2])
    out_ref[...] = jnp.where(lane_at < OWN, gains, best_column)


def local(features, labels, weights, nodes):
    dma = pltpu.SemaphoreType.DMA
    result = pl.pallas_call(
        kernel,
        out_shape=jax.ShapeDtypeStruct((8, 128), f32),
        in_specs=[pl.BlockSpec(memory_space=pl.ANY)] * 4,
        out_specs=pl.BlockSpec(memory_space=pltpu.VMEM),
        scratch_shapes=[
            pltpu.VMEM((512, LOCAL), f32),
            pltpu.VMEM((1, LOCAL), jnp.int32),
            pltpu.VMEM((1, LOCAL), bf16),
            pltpu.VMEM((1, LOCAL), jnp.int32),
            pltpu.VMEM((ROWS_AX, FEAT_AX + 1, 8, 128), bf16),
            pltpu.VMEM((ROWS_AX, FEAT_AX + 1, 8, 128), bf16),
            pltpu.VMEM((ROWS_AX, FEAT_AX, 2, 8, 128), bf16),
            pltpu.VMEM((OWN * B, NODES * C), f32),
            pltpu.VMEM((1, 128), f32),
            pltpu.VMEM((ROWS_AX, FEAT_AX, 1, 128), f32),
            pltpu.SemaphoreType.REGULAR((len(LEVELS) - 1, 2)),
            dma((CHUNKS + 3,)), dma(()), dma((ROWS_AX,)), dma(()), dma((ROWS_AX,)), dma(()), dma(()), dma(()), dma(()),
        ],
        compiler_params=pltpu.CompilerParams(collective_id=0, has_side_effects=True, vmem_limit_bytes=48 * 1024 * 1024),
        name="split_scores",
    )(*[pltpu.with_memory_space_constraint(v, pltpu.HBM) for v in (features, labels.reshape(1, -1), weights, nodes)])
    return result[None, :NODES, :OWN], jnp.max(result[None, :NODES, OWN : 2 * OWN], axis=2)


def solution(mesh):
    return jax.shard_map(
        local,
        mesh=mesh,
        in_specs=(
            P(None, ("rows", "feat")),
            P(("rows", "feat")),
            P("leaf", ("rows", "feat")),
            P("leaf", ("rows", "feat")),
        ),
        out_specs=(P("leaf", None, ("rows", "feat")), P("leaf", None)),
        check_vma=False,
    )
```

```python
import jax
import jax.numpy as jnp
from jax import lax
from jax.experimental import pallas as pl
from jax.experimental.pallas import tpu as pltpu
from jax.sharding import PartitionSpec as P

B = 128
C = 64
NODES = 2
OWN = 4
Z = 8
Y = 2
X = 4
CORES = 2
ROWS_AX = Z * Y
CHUNKS = 4
FEAT_AX = X * CORES
LOCAL = 256
f32 = jnp.float32
bf16 = jnp.bfloat16
MESH = pl.DeviceIdType.MESH
NT = (((1,), (1,)), ((), ()))
ORDER = [(0, 0), (0, 1), (1, 0), (7, 0), (1, 1), (7, 1), (2, 0), (6, 0), (2, 1), (6, 1), (3, 0), (5, 0), (3, 1), (5, 1), (4, 0), (4, 1)]
NEAR = 6


def bin_index(x):
    guess = jnp.clip(jnp.ceil(x * (B / 9.0) + (B // 2 - 1)), 0.0, B - 1.0)
    edge_here = (guess + (1.0 - B // 2)) * (9.0 / B)
    edge_before = (guess - (1.0 * (B // 2))) * (9.0 / B)
    up = jnp.where((edge_here < x) & (guess < B - 1.0), 1.0, 0.0)
    down = jnp.where((edge_before >= x) & (guess > 0.0), 1.0, 0.0)
    return guess + up - down


def row_pack(tile, row):
    return jnp.broadcast_to(tile[row : row + 1, :], (16, 128)).astype(bf16)


def mask_tile(tile, bins):
    one, zero = jnp.ones((), bf16), jnp.zeros((), bf16)
    rows = []
    for i in range(OWN):
        halves = []
        for h in range(2):
            packed = row_pack(tile, h * 4 + i)
            halves.append(jnp.where(packed[None] <= bins, one, zero).reshape(B, 128))
        rows.append(jnp.concatenate(halves, axis=1))
    return jnp.concatenate(rows, axis=0)


def target_tile(tile, classes):
    zero = jnp.zeros((), bf16)
    parts = [[], []]
    for h in range(2):
        hit = row_pack(tile, h * 4)[None] == classes
        for n in range(NODES):
            weight = jnp.broadcast_to(row_pack(tile, h * 4 + 1 + n)[None], hit.shape)
            parts[n].append(jnp.where(hit, weight, zero).reshape(C, 128))
    return jnp.concatenate([jnp.concatenate(p, axis=1) for p in parts], axis=0)


def ratio(values):
    return jnp.sum(values * values, axis=0, keepdims=True) / jnp.maximum(jnp.sum(values, axis=0, keepdims=True), 1.0)


def kernel(
    feat_hbm, lab_hbm, wei_hbm, node_hbm, out_ref,
    feat_v, lab_v, wei_v, node_v, send, own_codes, rbuf, acc, top_row, tops,
    in_sem, feat_recv, code_recv, far_recv, top_recv, sent,
):
    my_rows, my_feat = lax.axis_index("rows"), lax.axis_index("feat")
    z, y = lax.div(my_rows, Y), lax.rem(my_rows, Y)

    def rows_peer(s):
        dz, dy = ORDER[s]
        return lax.rem(z + dz, Z) * Y + lax.rem(y + dy, Y)

    def feat_peer(d):
        return lax.rem(my_feat + d, FEAT_AX)

    def to_column(s, action):
        rows = rows_peer(s)

        def one(d, carry):
            action(rows, feat_peer(d), d)
            return carry

        lax.fori_loop(1 if s == 0 else 0, FEAT_AX, one, 0)

    def push(source, target, send_sem, recv_sem, rows, feat):
        pltpu.make_async_remote_copy(
            src_ref=source, dst_ref=target, send_sem=send_sem, recv_sem=recv_sem,
            device_id={"rows": rows, "feat": feat}, device_id_type=MESH).start()

    def wait_all(part, sem):
        pltpu.make_async_copy(part, part, sem).wait()

    loads = [
        pltpu.make_async_copy(lab_hbm, lab_v, in_sem.at[CHUNKS]),
        pltpu.make_async_copy(wei_hbm, wei_v, in_sem.at[CHUNKS + 1]),
        pltpu.make_async_copy(node_hbm, node_v, in_sem.at[CHUNKS + 2]),
    ]
    chunk_loads = []
    for q in range(CHUNKS):
        part = pl.ds(q * (512 // CHUNKS), 512 // CHUNKS)
        chunk_loads.append(pltpu.make_async_copy(feat_hbm.at[part], feat_v.at[part], in_sem.at[q]))
    for load in loads + chunk_loads:
        load.start()

    barrier = pltpu.get_barrier_semaphore()

    def greet(rows, feat, d):
        pl.semaphore_signal(barrier, inc=1, device_id={"rows": rows, "feat": feat}, device_id_type=MESH)

    for s in reversed(range(ROWS_AX)):
        to_column(s, greet)
    for load in loads:
        load.wait()

    label = lab_v[...].astype(f32)
    weight = wei_v[...].astype(f32)
    node = node_v[...]
    w0 = jnp.where(node == 0, weight, 0.0)
    w1 = jnp.where(node == 1, weight, 0.0)
    pad = jnp.zeros_like(w0)
    lines = []
    for h in range(2):
        cut = slice(h * 128, (h + 1) * 128)
        lines += [label[:, cut], w0[:, cut], w1[:, cut], pad[:, cut]]
    codes = jnp.concatenate(lines, axis=0).astype(bf16)
    sub = lax.broadcasted_iota(jnp.int32, (4, 8, 128), 1)

    def binned(r):
        values = bin_index(feat_v[pl.ds(pl.multiple_of(r * 32, 32), 32), :])
        a = values[:, :128].reshape(4, 8, 128)
        b = values[:, 128:].reshape(4, 8, 128)
        first = jnp.where(sub < 4, a, pltpu.roll(b, 4, 1))
        second = jnp.where(sub < 4, pltpu.roll(a, 4, 1), b)
        return jnp.stack([first, second], axis=1).reshape(8, 8, 128).astype(bf16)

    def place(r, carry):
        send[r] = binned(r)
        return carry

    own_codes[...] = codes
    rbuf[0, 0, 1] = codes
    for q in range(CHUNKS):
        chunk_loads[q].wait()
        lax.fori_loop(q * (ROWS_AX // CHUNKS), (q + 1) * (ROWS_AX // CHUNKS), place, 0)
    rbuf[0, 0, 0] = send[my_rows, my_feat]
    acc[...] = jnp.zeros_like(acc)

    bins = (lax.broadcasted_iota(jnp.int32, (8, 16, 128), 0) * 16 + lax.broadcasted_iota(jnp.int32, (8, 16, 128), 1)).astype(f32).astype(bf16)
    classes = bins[: C // 16]

    def use(start, count):
        masks, targets = [], []
        for u in range(count):
            s = start + u
            for d in range(FEAT_AX):
                masks.append(mask_tile(rbuf[s, d, 0].astype(f32), bins))
                targets.append(target_tile(rbuf[s, d, 1].astype(f32), classes))
        acc[...] += lax.dot_general(jnp.concatenate(masks, axis=1), jnp.concatenate(targets, axis=1), NT, preferred_element_type=f32)

    others = pl.ds(1, FEAT_AX - 1)

    def push_features(s):
        def one(rows, feat, d):
            push(send.at[rows, feat], rbuf.at[s, d, 0], sent.at[0 if s == 0 else 1], feat_recv.at[s], rows, feat)

        to_column(s, one)

    def push_codes(s):
        def one(rows, feat, d):
            push(own_codes, rbuf.at[s, d, 1], sent.at[2 if s == 0 else 3], code_recv.at[s], rows, feat)

        to_column(s, one)

    pl.semaphore_wait(barrier, ROWS_AX * FEAT_AX - 1)
    for s in range(NEAR):
        push_codes(s)
        push_features(s)
        if s == 1:
            for far in range(NEAR, ROWS_AX):
                push(own_codes, rbuf.at[far, 0, 1], sent.at[4], far_recv.at[far], rows_peer(far), my_feat)
    for s in range(NEAR, ROWS_AX):
        push_features(s)

    wait_all(rbuf.at[0, others, 0], feat_recv.at[0])
    wait_all(rbuf.at[0, others, 1], code_recv.at[0])
    wait_all(rbuf.at[1, :, 0], feat_recv.at[1])
    wait_all(rbuf.at[1, :, 1], code_recv.at[1])
    use(0, 2)

    def pass_on(s, carry):
        wait_all(rbuf.at[s, 0, 1], far_recv.at[s])

        def one(d, inner):
            push(rbuf.at[s, 0, 1], rbuf.at[s, d, 1], sent.at[5], code_recv.at[s], my_rows, feat_peer(d))
            return inner

        lax.fori_loop(1, FEAT_AX, one, 0)
        return carry

    lax.fori_loop(NEAR, ROWS_AX, pass_on, 0)

    def step(g, carry):
        for u in range(2):
            s = 2 * g + u
            wait_all(rbuf.at[s, :, 0], feat_recv.at[s])

            @pl.when(g < NEAR // 2)
            def _():
                wait_all(rbuf.at[s, :, 1], code_recv.at[s])

            @pl.when(g >= NEAR // 2)
            def _():
                wait_all(rbuf.at[s, others, 1], code_recv.at[s])

        use(2 * g, 2)
        return carry

    lax.fori_loop(1, ROWS_AX // 2, step, 0)

    row_at = lax.broadcasted_iota(jnp.int32, (8, 128), 0)
    lane_at = lax.broadcasted_iota(jnp.int32, (8, 128), 1)
    gains = jnp.zeros((8, 128), f32)
    best = jnp.zeros((1, 128), f32)
    lane_row = lax.broadcasted_iota(jnp.int32, (1, 128), 1)
    for n in range(NODES):
        node_top = None
        for i in range(OWN):
            left = acc[i * B : (i + 1) * B, :].T[n * C : (n + 1) * C, :]
            total = left[:, B - 1 : B]
            right = total - left
            gain = ratio(left) + ratio(right) - ratio(total)
            top = jnp.max(gain, axis=1, keepdims=True)
            gains = jnp.where((row_at == n) & (lane_at == i), top, gains)
            node_top = top if node_top is None else jnp.maximum(node_top, top)
        best = jnp.where(lane_row == n, node_top, best)

    top_row[0] = best

    def push_near(d, carry):
        push(top_row.at[0], tops.at[0, d], sent.at[6], top_recv.at[0], my_rows, feat_peer(d))
        return carry

    lax.fori_loop(1, FEAT_AX, push_near, 0)
    wait_all(tops.at[0, others], top_recv.at[0])
    best = jnp.maximum(best, jnp.max(tops[0, 1:], axis=0))
    top_row[1] = best
    for s in reversed(range(1, ROWS_AX)):
        push(top_row.at[1], tops.at[s, 0], sent.at[7], top_recv.at[1], rows_peer(s), my_feat)
    rest, far_rest = pl.ds(1, ROWS_AX - 1), pl.ds(NEAR, ROWS_AX - NEAR)
    wait_all(rbuf.at[0, others, 0], sent.at[0])
    wait_all(rbuf.at[rest, :, 0], sent.at[1])
    wait_all(rbuf.at[0, others, 1], sent.at[2])
    wait_all(rbuf.at[pl.ds(1, NEAR - 1), :, 1], sent.at[3])
    wait_all(rbuf.at[far_rest, 0, 1], sent.at[4])
    wait_all(rbuf.at[far_rest, others, 1], sent.at[5])
    wait_all(tops.at[0, others], sent.at[6])
    wait_all(tops.at[rest, 0], sent.at[7])
    wait_all(tops.at[rest, 0], top_recv.at[1])
    best = jnp.maximum(best, jnp.max(tops[1:, 0], axis=0))
    best_column = jnp.where(row_at == 0, best[:, 0:1], best[:, 1:2])
    out_ref[...] = jnp.where(lane_at < OWN, gains, best_column)


def local(features, labels, weights, nodes):
    dma = pltpu.SemaphoreType.DMA
    result = pl.pallas_call(
        kernel,
        out_shape=jax.ShapeDtypeStruct((8, 128), f32),
        in_specs=[pl.BlockSpec(memory_space=pl.ANY)] * 4,
        out_specs=pl.BlockSpec(memory_space=pltpu.VMEM),
        scratch_shapes=[
            pltpu.VMEM((512, LOCAL), f32),
            pltpu.VMEM((1, LOCAL), jnp.int32),
            pltpu.VMEM((1, LOCAL), bf16),
            pltpu.VMEM((1, LOCAL), jnp.int32),
            pltpu.VMEM((ROWS_AX, FEAT_AX, 8, 128), bf16),
            pltpu.VMEM((8, 128), bf16),
            pltpu.VMEM((ROWS_AX, FEAT_AX, 2, 8, 128), bf16),
            pltpu.VMEM((OWN * B, NODES * C), f32),
            pltpu.VMEM((2, 1, 128), f32),
            pltpu.VMEM((ROWS_AX, FEAT_AX, 1, 128), f32),
            dma((CHUNKS + 3,)), dma((ROWS_AX,)), dma((ROWS_AX,)), dma((ROWS_AX,)), dma((2,)), dma((8,)),
        ],
        compiler_params=pltpu.CompilerParams(collective_id=0, has_side_effects=True, vmem_limit_bytes=48 * 1024 * 1024),
        name="split_scores",
    )(*[pltpu.with_memory_space_constraint(v, pltpu.HBM) for v in (features, labels.reshape(1, -1), weights, nodes)])
    return result[None, :NODES, :OWN], jnp.max(result[None, :NODES, OWN : 2 * OWN], axis=2)


def solution(mesh):
    return jax.shard_map(
        local,
        mesh=mesh,
        in_specs=(
            P(None, ("rows", "feat")),
            P(("rows", "feat")),
            P("leaf", ("rows", "feat")),
            P("leaf", ("rows", "feat")),
        ),
        out_specs=(P("leaf", None, ("rows", "feat")), P("leaf", None)),
        check_vma=False,
    )
```
